128 devices in a mesh: rep: 4 (over z), ep: 32 (over y, x, core).
Axes of the slice: x: 4, y: 4, z: 4, core: 2. Of those that a mesh axis runs over, the one named last changes fastest.
Arguments:
- tokens: bfloat16 [16384, 2048], P(('rep', 'ep')), may hold values from -6 to 6
- experts: int32 [16384, 10], P(('rep', 'ep')), may hold values from 0 to 127, all different within a row; in each aligned block of 128 rows (0 to 127, 128 to 255, ...) at most 16 rows name the same one
- gates: bfloat16 [16384, 10], P(('rep', 'ep')), may hold values from 0.099609375 to 0.5
- w_gate: bfloat16 [128, 2048, 512], P('ep'), may hold values from -0.125 to 0.125
- w_up: bfloat16 [128, 2048, 512], P('ep'), may hold values from -0.125 to 0.125
- w_down: bfloat16 [128, 2048, 512], P('ep'), may hold values from -0.25 to 0.25
Outputs:
- mixed: bfloat16 [16384, 2048], P(('rep', 'ep'))
The draws below stay inside these ranges and needn't reach their ends.
Inputs may be any that keep to these rules, and one draw needn't show every extreme that they name: Each row names 10 different experts. Among the 128 tokens of one device (aligned blocks of rows), no expert is named more than 16 times; in some such blocks one expert is named exactly 16 times.
All inputs are finite; a program needn't handle non-finite values.
Results may differ from the reference program's by a relative error of at most 0.0057.
Values may be sent and summed in bfloat16 or wider, within the bound.
A program may use at most 128 MiB of HBM per device.

```python
import math
import jax
import jax.numpy as jnp
import numpy as np
from jax import lax

D = 2048
FF = 512
TOPK = 10
TOK_DEV = 128
EXPERTS = 128
CAP = 16
TOKENS = 16384
DEVICES = 128


def steps_of(stream_key, extent, cuts, smallest, largest):
    gain, own = 1.0, jax.random.fold_in(stream_key, 6)
    for axis_at, parts in cuts:
        heights = jnp.exp(jax.random.uniform(jax.random.fold_in(own, axis_at), (parts,), jnp.float32, smallest / len(cuts), largest / len(cuts)))
        gain = gain * jnp.repeat(heights, extent[axis_at] // parts).reshape([-1 if axis == axis_at else 1 for axis in range(len(extent))])
    return gain


def deal_out(rng, own, number, rows, number_of, top, bound, slope):
    sequence = jax.random.permutation(rng, number_of)
    packed, usual = portions_of(number_of, rows * top, bound, slope, True), portions_of(number_of, rows * top, bound, slope, False)
    places = jnp.arange(number_of)

    def named(tallies, rotation):
        used = int((tallies > 0).sum())
        fixed = max(1, used // 4)
        passed = fixed + (places - fixed + rotation * (used - fixed)) % max(1, number_of - fixed)
        return jnp.zeros((number_of,), jnp.int32).at[sequence[jnp.where(places < fixed, places, passed)]].set(jnp.asarray(tallies, jnp.int32))

    tallies = jnp.where(number % 4 == 0, named(packed, number // 4), named(usual, number - number // 4 - 1))
    mixed = jax.random.permutation(jax.random.fold_in(own, 3), number_of)
    giver, receiver = mixed[0:number_of // 2 * 2:2], mixed[1:number_of // 2 * 2:2]
    margin = jnp.minimum(tallies[giver] - 1, bound - tallies[receiver]) // 2
    margin = jnp.where((giver == sequence[0]) | (receiver == sequence[0]) | (tallies[receiver] == 0), 0, jnp.maximum(margin, 0))
    passed = jax.random.randint(jax.random.fold_in(own, 4), (number_of // 2,), 0, 1 << 20) % (margin + 1)
    tallies = tallies.at[giver].add(-passed).at[receiver].add(passed)
    members = jnp.searchsorted(jnp.cumsum(tallies), jnp.arange(rows * top), side="right").astype(jnp.int32)
    listing = members.reshape(top, rows).T
    listing = listing[jax.random.permutation(jax.random.fold_in(own, 1), rows)]
    rotation = jax.random.randint(jax.random.fold_in(own, 2), (rows, 1), 0, top)
    return jnp.take_along_axis(listing, (jnp.arange(top)[None, :] + rotation) % top, axis=1)


def portions_of(number_of, total, bound, skew, full):
    portions = [(1 << 20) // math.isqrt(rank ** skew) + 1 for rank in range(1, number_of + 1)]
    largest = bound if full else min(bound, max(-(-total // number_of), total * portions[0] // sum(portions)))
    least = 1 if total - largest >= number_of - 1 else 0
    given, spare = [largest] + [least] * (number_of - 1), total - largest - least * (number_of - 1)
    while spare > 0:
        movable = [i for i in range(1, number_of) if given[i] < largest] or [i for i in range(1, number_of) if given[i] < bound]
        whole, remaining = sum([portions[i] for i in movable]), spare
        for i in movable:
            addition = min(bound - given[i], max(1, remaining * portions[i] // whole), spare)
            given[i] = given[i] + addition
            spare = spare - addition
    return np.array(given)


def bell_draw(stream_key, extent, spread, reach, shards=(), held_as=jnp.bfloat16):
    drawn = jax.random.normal(stream_key, extent, jnp.float32) * spread
    if len(shards) > 0:
        drawn = steps_of(stream_key, extent, shards, -0.22, 0.18) * drawn
    return jnp.clip(drawn, min=-reach, max=reach).astype(held_as)


def setup_inputs(seed: int = 0) -> dict:
    splits = jax.random.split(jax.random.key(seed), 7)
    tokens = bell_draw(splits[0], (TOKENS, D), 1.0, 6.0, ((0, 128),))
    experts_keys = jax.random.split(jax.random.fold_in(splits[1], 1), TOKENS // TOK_DEV)
    experts_turns = jax.random.permutation(jax.random.fold_in(splits[1], 3), TOKENS // TOK_DEV)
    experts = jax.vmap(lambda own, number: deal_out(jax.random.fold_in(splits[1], 2), own, number, TOK_DEV, EXPERTS, TOPK, CAP, 2))(experts_keys, experts_turns).reshape((TOKENS, TOPK))
    gates = jnp.clip(0.099609375 + 0.40039062 * jax.random.uniform(splits[2], (TOKENS, TOPK), jnp.float32) ** steps_of(splits[2], (TOKENS, TOPK), ((0, 128),), -0.2, 0.2), 0.099609375, 0.5).astype(jnp.bfloat16)
    w_gate = bell_draw(splits[3], (EXPERTS, D, FF), D ** -0.5, 0.125, ((0, 32),))
    w_up = bell_draw(splits[4], (EXPERTS, D, FF), D ** -0.5, 0.125, ((0, 32),))
    w_down = bell_draw(splits[5], (EXPERTS, D, FF), FF ** -0.5, 0.25, ((0, 32),))
    return {"tokens": tokens, "experts": experts, "gates": gates, "w_gate": w_gate, "w_up": w_up, "w_down": w_down}


def reference(tokens, experts, gates, w_gate, w_up, w_down):
    flat = experts.reshape(DEVICES, TOK_DEV * TOPK)
    onehot = (flat[:, :, None] == jnp.arange(EXPERTS, dtype=jnp.int32)[None, None, :]).astype(jnp.int32)
    position = jnp.sum(jnp.cumsum(onehot, axis=1) * onehot, axis=-1) - 1
    rows_each = DEVICES * CAP
    owner = jnp.arange(DEVICES, dtype=jnp.int32)[:, None]
    slot = (flat * rows_each + owner * CAP + position).reshape(-1).astype(jnp.int32)
    token_ids = (jnp.arange(DEVICES * TOK_DEV * TOPK, dtype=jnp.int32) // TOPK).astype(jnp.int32)
    table = jnp.zeros((EXPERTS * rows_each,), jnp.int32).at[slot].set(token_ids).reshape(EXPERTS, rows_each)
    weights = jnp.zeros((EXPERTS * rows_each,), jnp.float32).at[slot].set(gates.reshape(-1).astype(jnp.float32)).reshape(EXPERTS, rows_each)

    def one_expert(total, index):
        picked = tokens[table[index]]
        gate_act = jnp.dot(picked, w_gate[index], preferred_element_type=jnp.float32)
        up_act = jnp.dot(picked, w_up[index], preferred_element_type=jnp.float32)
        hidden = (jax.nn.silu(gate_act) * up_act).astype(jnp.bfloat16)
        result = jnp.dot(hidden, w_down[index].T, preferred_element_type=jnp.float32).astype(jnp.bfloat16)
        contrib = result.astype(jnp.float32) * weights[index][:, None]
        return total.at[table[index]].add(contrib), None

    start = jnp.zeros((TOKENS, D), jnp.float32)
    total, unused = lax.scan(one_expert, start, jnp.arange(EXPERTS, dtype=jnp.int32))
    return total.astype(jnp.bfloat16)
```

```python
import jax
import jax.numpy as jnp
from jax import lax
from jax.experimental import pallas as pl
from jax.experimental.pallas import tpu as pltpu
from jax.sharding import PartitionSpec as P

MESH = pl.DeviceIdType.MESH
F32, BF16 = jnp.float32, jnp.bfloat16
SIDE = 4
WIDTH, HIDDEN, TOKS, CAP, HELD = 2048, 512, 128, 16, 4
BODY, META = 1024, 16
ROWS = BODY + META
SPANS = {"f": (0, ROWS), "t": (0, 528), "b": (528, 512)}
RET = {"f": (0, BODY), "t": (0, 512), "b": (512, 512)}
ORDER = [(0, 0), (1, 0), (3, 0), (0, 1), (0, 3), (2, 0), (0, 2), (1, 1),
         (1, 3), (3, 1), (3, 3), (2, 1), (2, 3), (1, 2), (3, 2), (2, 2)]
SLOT = {d: i for i, d in enumerate(ORDER)}
CHUNK = 4
N_CHUNKS = len(ORDER) // CHUNK
SRC = 2 * CHUNK


def slot(h, df, dg):
    return SLOT[(df, dg)] if h == 0 else SLOT[(dg, df)]


def kernel(tok_hbm, meta_ref, wg_hbm, wu_hbm, wd_hbm, out_ref,
           g, p, wg, wu, wd, xb, ws, ps,
           own_sem, w_sem, ds, dr, xs, xr, ys, yr, rs, rr, free_sem, ready_sem):
    me = lax.axis_index("ep")
    core, x, y = me % 2, (me // 2) % SIDE, me // (2 * SIDE)

    def at(cx, cy, c):
        return (cy * SIDE + cx) * 2 + c

    nbr = {
        ("x", 1): at((x + 1) % SIDE, y, core),
        ("x", -1): at((x + SIDE - 1) % SIDE, y, core),
        ("y", 1): at(x, (y + 1) % SIDE, core),
        ("y", -1): at(x, (y + SIDE - 1) % SIDE, core),
    }
    mate = at(x, y, 1 - core)
    first, second = ("x", "y"), ("y", "x")

    own = []
    for h in range(2):
        for c in range(8):
            own.append(pltpu.make_async_copy(
                tok_hbm.at[:, pl.ds((h * 8 + c) * 128, 128)],
                g.at[0, 0, h, pl.ds(c * 128, 128), :], own_sem.at[h * 9 + c]))
        own.append(pltpu.make_async_copy(
            meta_ref.at[h], g.at[0, 0, h, pl.ds(BODY, META), :], own_sem.at[h * 9 + 8]))
    for c in own:
        c.start()
    loads = []
    for e in range(HELD):
        for i, (src, dst) in enumerate(((wg_hbm, wg), (wu_hbm, wu), (wd_hbm, wd))):
            loads.append(pltpu.make_async_copy(src.at[e], dst.at[e], w_sem.at[e * 3 + i]))
    for c in loads:
        c.start()

    barrier = pltpu.get_barrier_semaphore()
    for n in (*nbr.values(), mate):
        pl.semaphore_signal(barrier, inc=1, device_id={"ep": n}, device_id_type=MESH)
    pl.semaphore_wait(barrier, 5)
    for c in own:
        c.wait()

    ids, out_copies, pending_out = {}, {}, []

    def go(h, df, dg, part):
        key = (h, df, dg, part)
        ids[key] = i = len(ids)
        axis, d = (first[h], df) if dg == 0 else (second[h], dg)
        step = 1 if (d == 3 or part == "t") else -1
        prev = (d + step) % SIDE
        s = slot(h, prev, 0) if dg == 0 else slot(h, df, prev)
        a, n = SPANS[part]
        copy = pltpu.make_async_remote_copy(
            src_ref=g.at[0, s, h, pl.ds(a, n), :], dst_ref=g.at[0, slot(h, df, dg), h, pl.ds(a, n), :],
            send_sem=ds.at[i], recv_sem=dr.at[i],
            device_id={"ep": nbr[axis, step]}, device_id_type=MESH)
        copy.start()
        out_copies[key] = copy

    cross = {}

    def share(h, s):
        copy = pltpu.make_async_remote_copy(
            src_ref=g.at[0, s, h], dst_ref=g.at[1, s, h], send_sem=xs.at[h, s], recv_sem=xr.at[h, s],
            device_id={"ep": mate}, device_id_type=MESH)
        copy.start()
        cross[h, s] = copy

    def second_ring(h, df):
        go(h, df, 3, "f")
        go(h, df, 1, "f")

    def arrive(df, dg):
        for h in range(2):
            far = (df if dg == 0 else dg) == 2
            for part in ("t", "b") if far else ("f",):
                out_copies[h, df, dg, part].wait_recv()
            if dg == 0:
                if not far:
                    go(h, 2, 0, "t" if df == 3 else "b")
                second_ring(h, df)
            elif not far:
                go(h, df, 2, "t" if dg == 3 else "b")
            share(h, slot(h, df, dg))

    for h in range(2):
        go(h, 3, 0, "f")
        go(h, 1, 0, "f")
    for h in range(2):
        second_ring(h, 0)
    for h in range(2):
        share(h, 0)

    row_i = lax.broadcasted_iota(jnp.int32, (TOKS, TOKS), 0)
    col_i = lax.broadcasted_iota(jnp.int32, (TOKS, TOKS), 1)
    before = (row_i < col_i).astype(F32).astype(BF16)
    cap_i = lax.broadcasted_iota(jnp.int32, (CAP, TOKS), 0).astype(F32)
    back = {}

    def chunk(c):
        base = c * CHUNK
        for s in range(base, base + CHUNK):
            for h in range(2):
                cross[h, s].wait_recv()

        def route(i, carry):
            o, l = base + i // 2, i % 2
            chosen = g[l, o, 0, pl.ds(BODY, META), :].astype(F32)
            gate = g[l, o, 1, pl.ds(BODY, META), :].astype(F32)
            for e in range(HELD):
                mine = (me * HELD + e).astype(F32)
                ws[i, pl.ds(e, 1), :] = jnp.sum(jnp.where(chosen == mine, gate, 0.0), axis=0, keepdims=True)
            w = ws[i]
            rank = jnp.dot((w > 0.0).astype(F32).astype(BF16), before, preferred_element_type=F32)
            ps[i] = jnp.where(w > 0.0, rank, -1.0)
            r = ps[i]
            spread = jnp.concatenate(
                [jnp.where(jnp.broadcast_to(r[e:e + 1], (CAP, TOKS)) == cap_i, 1.0, 0.0) for e in range(HELD)],
                axis=0).astype(BF16)
            rows = pl.ds(pl.multiple_of(i * CAP, CAP), CAP)
            for j in range(8):
                h, k = j // 4, (j % 4) * 2
                pair = jnp.concatenate(
                    [g[l, o, h, pl.ds(k * 128, 128), :], g[l, o, h, pl.ds(k * 128 + 128, 128), :]], axis=1)
                picked = jnp.dot(spread, pair, preferred_element_type=F32).astype(BF16)
                for e in range(HELD):
                    xb[e, rows, pl.ds(j * 256, 256)] = picked[e * CAP:(e + 1) * CAP]
            return carry

        ws[...] = jnp.zeros_like(ws)
        lax.fori_loop(0, SRC, route, 0)
        pl.semaphore_signal(free_sem.at[c], inc=1, device_id={"ep": mate}, device_id_type=MESH)

        def expert(e, carry):
            rows = xb[e]
            gate_act = jnp.dot(rows, wg[e], preferred_element_type=F32)
            up_act = jnp.dot(rows, wu[e], preferred_element_type=F32)
            hidden = (gate_act / (1.0 + jnp.exp(-gate_act)) * up_act).astype(BF16)
            for j in range(4):
                xb[e, :, pl.ds(j * 512, 512)] = lax.dot_general(
                    hidden, wd[e, pl.ds(j * 512, 512), :], (((1,), (1,)), ((), ())),
                    preferred_element_type=F32).astype(BF16)
            return carry

        lax.fori_loop(0, HELD, expert, 0)

        def combine(i, carry):
            o, l = base + i // 2, i % 2
            r, w = ps[i], ws[i]
            mix = jnp.concatenate(
                [jnp.where(jnp.broadcast_to(r[e:e + 1], (CAP, TOKS)) == cap_i,
                           jnp.broadcast_to(w[e:e + 1], (CAP, TOKS)), 0.0) for e in range(HELD)], axis=0)
            mix = jnp.transpose(mix).astype(BF16)
            rows = pl.ds(pl.multiple_of(i * CAP, CAP), CAP)
            for j in range(8):
                h, k = j // 4, (j % 4) * 2
                res = jnp.concatenate([xb[e, rows, pl.ds(j * 256, 256)] for e in range(HELD)], axis=0)
                part = jnp.dot(mix, res, preferred_element_type=F32).astype(BF16)
                p[l, o, h, pl.ds(k * 128, 128), :] = part[:, :128]
                p[l, o, h, pl.ds(k * 128 + 128, 128), :] = part[:, 128:]
            return carry

        lax.fori_loop(0, SRC, combine, 0)
        pl.semaphore_wait(free_sem.at[c], 1)
        for s in range(base, base + CHUNK):
            copy = pltpu.make_async_remote_copy(
                src_ref=p.at[1, s], dst_ref=g.at[1, s, :, pl.ds(0, BODY), :],
                send_sem=ys.at[s], recv_sem=yr.at[s], device_id={"ep": mate}, device_id_type=MESH)
            copy.start()
            back[s] = copy

    arrive(1, 0)
    arrive(3, 0)
    arrive(0, 1)
    arrive(0, 3)
    for c in loads:
        c.wait()
    chunk(0)
    arrive(2, 0)
    arrive(1, 1)
    arrive(3, 1)
    arrive(1, 3)
    arrive(3, 3)
    arrive(0, 2)
    chunk(1)
    arrive(2, 1)
    arrive(1, 2)
    arrive(2, 3)
    chunk(2)
    arrive(3, 2)
    arrive(2, 2)
    chunk(3)

    for copy in (*out_copies.values(), *cross.values()):
        copy.wait_send()
    for n in nbr.values():
        pl.semaphore_signal(ready_sem, inc=1, device_id={"ep": n}, device_id_type=MESH)
    pl.semaphore_wait(ready_sem, 4)

    homes = {}

    def home(h, phase, df, kind):
        i = len(homes)
        axis = second[h] if phase == 1 else first[h]
        step = 1 if kind in "tp" else -1
        d = {"t": 2, "b": 2, "p": 1, "m": 3}[kind]
        s = slot(h, df, d) if phase == 1 else slot(h, d, 0)
        a, n = RET[kind if kind in "tb" else "f"]
        land = (df * 3 if phase == 1 else 12) + {"t": 0, "b": 0, "p": 1, "m": 2}[kind]
        copy = pltpu.make_async_remote_copy(
            src_ref=p.at[0, s, h, pl.ds(a, n), :], dst_ref=g.at[0, land, h, pl.ds(a, n), :],
            send_sem=rs.at[i], recv_sem=rr.at[i],
            device_id={"ep": nbr[axis, step]}, device_id_type=MESH)
        copy.start()
        homes[h, phase, df, kind] = copy

    came = set()

    def total(h, s, lands, mate_too=True):
        if mate_too and s not in came:
            back[s].wait_recv()
            came.add(s)
        for part in ("t", "b"):
            a, n = RET[part]
            terms = [k for k, span in lands if span in ("f", part)]
            if not mate_too and not terms:
                continue

            def add(i, carry):
                rows = pl.ds(pl.multiple_of(a + i * 128, 128), 128)
                v = p[0, s, h, rows, :].astype(F32)
                if mate_too:
                    v = v + g[1, s, h, rows, :].astype(F32)
                for k in terms:
                    v = v + g[0, k, h, rows, :].astype(F32)
                p[0, s, h, rows, :] = v.astype(BF16)
                return carry

            lax.fori_loop(0, n // 128, add, 0)

    def near(h, df):
        homes[h, 1, df, "t"].wait_recv()
        total(h, slot(h, df, 1), [(df * 3, "t")])
        home(h, 1, df, "p")
        homes[h, 1, df, "b"].wait_recv()
        total(h, slot(h, df, 3), [(df * 3, "b")])
        home(h, 1, df, "m")

    def column(h, df, more=()):
        homes[h, 1, df, "p"].wait_recv()
        homes[h, 1, df, "m"].wait_recv()
        total(h, slot(h, df, 0), [(df * 3 + 1, "f"), (df * 3 + 2, "f"), *more])

    for df in (2, 1, 3, 0):
        for h in range(2):
            total(h, slot(h, df, 2), [])
            home(h, 1, df, "t")
            home(h, 1, df, "b")
    for df in (2, 1, 3):
        for h in range(2):
            near(h, df)
    for h in range(2):
        column(h, 2)
        home(h, 2, 2, "t")
        home(h, 2, 2, "b")
    for h in range(2):
        near(h, 0)
    for h in range(2):
        homes[h, 2, 2, "t"].wait_recv()
        column(h, 1, [(12, "t")])
        home(h, 2, 1, "p")
        homes[h, 2, 2, "b"].wait_recv()
        column(h, 3, [(12, "b")])
        home(h, 2, 3, "m")
    for h in range(2):
        s = slot(h, 0, 0)
        for kind in ("p", "m"):
            homes[h, 1, 0, kind].wait_recv()
        homes[h, 2, 1, "p"].wait_recv()
        homes[h, 2, 3, "m"].wait_recv()
        if s not in came:
            back[s].wait_recv()
            came.add(s)
        for c in range(8):
            rows = pl.ds(c * 128, 128)
            v = p[0, s, h, rows, :].astype(F32) + g[1, s, h, rows, :].astype(F32)
            for k in (1, 2, 13, 14):
                v = v + g[0, k, h, rows, :].astype(F32)
            out_ref[:, pl.ds(h * BODY + c * 128, 128)] = v.astype(BF16)
    for copy in (*back.values(), *homes.values()):
        copy.wait_send()


def body(tokens, experts, gates, w_gate, w_up, w_down):
    chosen = jnp.pad(experts.astype(BF16).T, ((0, META - experts.shape[1]), (0, 0)), constant_values=-1)
    gate = jnp.pad(gates.T, ((0, META - gates.shape[1]), (0, 0)))
    meta = jnp.stack([chosen, gate])
    dma, any_spec = pltpu.SemaphoreType.DMA, pl.BlockSpec(memory_space=pl.ANY)
    vmem = pl.BlockSpec(memory_space=pltpu.VMEM)
    return pl.pallas_call(
        kernel,
        out_shape=jax.ShapeDtypeStruct((TOKS, WIDTH), BF16),
        in_specs=[any_spec, vmem, any_spec, any_spec, any_spec],
        out_specs=vmem,
        scratch_shapes=[
            pltpu.VMEM((2, 16, 2, ROWS, 128), BF16),
            pltpu.VMEM((2, 16, 2, BODY, 128), BF16),
            pltpu.VMEM((HELD, WIDTH, HIDDEN), BF16),
            pltpu.VMEM((HELD, WIDTH, HIDDEN), BF16),
            pltpu.VMEM((HELD, WIDTH, HIDDEN), BF16),
            pltpu.VMEM((HELD, SRC * CAP, WIDTH), BF16),
            pltpu.VMEM((SRC, 8, TOKS), F32),
            pltpu.VMEM((SRC, 8, TOKS), F32),
            dma((18,)), dma((12,)), dma((40,)), dma((40,)), dma((2, 16)), dma((2, 16)),
            dma((16,)), dma((16,)), dma((40,)), dma((40,)),
            pltpu.SemaphoreType.REGULAR((N_CHUNKS,)), pltpu.SemaphoreType.REGULAR,
        ],
        compiler_params=pltpu.CompilerParams(
            collective_id=0, has_side_effects=True, vmem_limit_bytes=67043328),
    )(tokens, meta, w_gate, w_up, w_down)


def solution(mesh):
    in_specs = (
        P(("rep", "ep"), None),
        P(("rep", "ep"), None),
        P(("rep", "ep"), None),
        P("ep", None, None),
        P("ep", None, None),
        P("ep", None, None),
    )
    out_specs = P(("rep", "ep"), None)
    return jax.shard_map(body, mesh=mesh, in_specs=in_specs, out_specs=out_specs, check_vma=False)
```

```python
import jax
import jax.numpy as jnp
from jax import lax
from jax.experimental import pallas as pl
from jax.experimental.pallas import tpu as pltpu
from jax.sharding import PartitionSpec as P

MESH = pl.DeviceIdType.MESH
F32, BF16 = jnp.float32, jnp.bfloat16
SIDE = 4
WIDTH, HIDDEN, TOKS, CAP, HELD = 2048, 512, 128, 16, 4
HALF = WIDTH // 2
BODY, META = 1024, 16
ROWS = BODY + META
SPANS = {"f": (0, ROWS), "t": (0, 528), "b": (528, 512)}
RET = {"f": (0, BODY), "t": (0, 512), "b": (512, 512)}
ORDER = [(0, 0), (1, 0), (3, 0), (0, 1), (0, 3), (1, 1), (1, 3), (3, 1),
         (3, 3), (2, 0), (0, 2), (2, 1), (2, 3), (1, 2), (3, 2), (2, 2)]
SLOT = {d: i for i, d in enumerate(ORDER)}
CHIPS = len(ORDER)


def kernel(tok_hbm, meta_ref, wg_hbm, wu_hbm, wd_hbm, out_hbm,
           g, p, wg, wu, wd, xb, ws, ps, fin,
           own_sem, w_sem, os_, or_, ds, dr, xs, xr, ys, yr, rs, rr, fs, fr, o_sem, free_sem, ready_sem):
    me = lax.axis_index("ep")
    core, x, y = me % 2, (me // 2) % SIDE, me // (2 * SIDE)
    other = 1 - core

    def at(cx, cy, c):
        return (cy * SIDE + cx) * 2 + c

    def pick(along_x, along_y):
        return other * along_x + core * along_y

    xp, xm = at((x + 1) % SIDE, y, core), at((x + SIDE - 1) % SIDE, y, core)
    yp, ym = at(x, (y + 1) % SIDE, core), at(x, (y + SIDE - 1) % SIDE, core)
    nbr = {("f", 1): pick(xp, yp), ("f", -1): pick(xm, ym), ("g", 1): pick(yp, xp), ("g", -1): pick(ym, xm)}
    mate = at(x, y, other)

    def remote(src, dst, send, recv, n):
        return pltpu.make_async_remote_copy(
            src_ref=src, dst_ref=dst, send_sem=send, recv_sem=recv, device_id={"ep": n}, device_id_type=MESH)

    own = []
    for k, half in ((0, core), (1, other)):
        for c in range(8):
            own.append(pltpu.make_async_copy(
                tok_hbm.at[:, pl.ds(pl.multiple_of(half * HALF + c * 128, 128), 128)],
                g.at[core, k, 0, pl.ds(c * 128, 128), :], own_sem.at[k * 9 + c]))
        own.append(pltpu.make_async_copy(
            meta_ref.at[half], g.at[core, k, 0, pl.ds(BODY, META), :], own_sem.at[k * 9 + 8]))
    for c in own:
        c.start()
    loads = []
    for e in range(HELD):
        for i, (src, dst) in enumerate(((wg_hbm, wg), (wu_hbm, wu), (wd_hbm, wd))):
            loads.append(pltpu.make_async_copy(src.at[e], dst.at[e], w_sem.at[e * 3 + i]))
    for c in loads:
        c.start()

    barrier = pltpu.get_barrier_semaphore()
    for n in (*nbr.values(), mate):
        pl.semaphore_signal(barrier, inc=1, device_id={"ep": n}, device_id_type=MESH)
    pl.semaphore_wait(barrier, 5)
    for c in own:
        c.wait()
    halves = [remote(g.at[core, 1 - k, 0], g.at[core, k, 0], os_.at[k], or_.at[k], mate) for k in range(2)]
    for c in halves:
        c.start()

    out_ids, sent, crossed = {}, {0: [], 1: []}, {0: [], 1: []}

    def leg(b, df, dg, part):
        i = out_ids.setdefault((df, dg, part), len(out_ids))
        axis, d = ("f", df) if dg == 0 else ("g", dg)
        step = 1 if (d == 3 or part == "t") else -1
        prev = (d + step) % SIDE
        s = SLOT[(prev, 0) if dg == 0 else (df, prev)]
        a, n = SPANS[part]
        return remote(g.at[b, 0, s, pl.ds(a, n), :], g.at[b, 0, SLOT[df, dg], pl.ds(a, n), :],
                      ds.at[b, i], dr.at[b, i], nbr[axis, step])

    def go(b, *key):
        copy = leg(b, *key)
        copy.start()
        sent[b].append(copy)

    def share(b, df, dg):
        return remote(g.at[b, 0, SLOT[df, dg]], g.at[b, 1, SLOT[dg, df]],
                      xs.at[b, SLOT[dg, df]], xr.at[b, SLOT[dg, df]], mate)

    def second_ring(b, df):
        go(b, df, 3, "f")
        go(b, df, 1, "f")

    def first_ring(b):
        go(b, 3, 0, "f")
        go(b, 1, 0, "f")

    def arrive(b, df, dg):
        far = (df if dg == 0 else dg) == 2
        for part in ("t", "b") if far else ("f",):
            leg(b, df, dg, part).wait_recv()
        if dg == 0:
            if not far:
                go(b, 2, 0, "t" if df == 3 else "b")
            second_ring(b, df)
        elif not far:
            go(b, df, 2, "t" if dg == 3 else "b")
        copy = share(b, df, dg)
        copy.start()
        crossed[b].append(copy)

    row_i = lax.broadcasted_iota(jnp.int32, (TOKS, TOKS), 0)
    col_i = lax.broadcasted_iota(jnp.int32, (TOKS, TOKS), 1)
    before = (row_i < col_i).astype(F32).astype(BF16)
    cap_i = lax.broadcasted_iota(jnp.int32, (CAP, TOKS), 0).astype(F32)

    def rows_of(s):
        return pl.ds(pl.multiple_of(s * CAP, CAP), CAP)

    def route(b, s0, n):
        for s in range(s0, s0 + n):
            if s > 0:
                df, dg = ORDER[s]
                share(b, dg, df).wait_recv()

        def one(s, carry):
            chosen = g[b, core, s, pl.ds(BODY, META), :].astype(F32)
            gate = g[b, other, s, pl.ds(BODY, META), :].astype(F32)
            for e in range(HELD):
                mine = (me * HELD + e).astype(F32)
                ws[s, pl.ds(e, 1), :] = jnp.sum(jnp.where(chosen == mine, gate, 0.0), axis=0, keepdims=True)
            w = ws[s]
            rank = jnp.dot((w > 0.0).astype(F32).astype(BF16), before, preferred_element_type=F32)
            r = jnp.where(w > 0.0, rank, -1.0)
            ps[s] = r
            spread = jnp.concatenate(
                [jnp.where(jnp.broadcast_to(r[e:e + 1], (CAP, TOKS)) == cap_i, 1.0, 0.0) for e in range(HELD)],
                axis=0).astype(BF16)
            for j in range(8):
                k, c = (j // 4 + core) % 2, (j % 4) * 2
                pair = jnp.concatenate(
                    [g[b, k, s, pl.ds(c * 128, 128), :], g[b, k, s, pl.ds(c * 128 + 128, 128), :]], axis=1)
                picked = jnp.dot(spread, pair, preferred_element_type=F32).astype(BF16)
                for e in range(HELD):
                    xb[e, rows_of(s), pl.ds(j * 256, 256)] = picked[e * CAP:(e + 1) * CAP]
            return carry

        lax.fori_loop(s0, s0 + n, one, 0)

    def expert(e0, n):
        def one(e, carry):
            rows = xb[e]
            gate_act = jnp.dot(rows, wg[e], preferred_element_type=F32)
            up_act = jnp.dot(rows, wu[e], preferred_element_type=F32)
            hidden = (gate_act / (1.0 + jnp.exp(-gate_act)) * up_act).astype(BF16)
            for j in range(4):
                xb[e, :, pl.ds(j * 512, 512)] = lax.dot_general(
                    hidden, wd[e, pl.ds(j * 512, 512), :], (((1,), (1,)), ((), ())),
                    preferred_element_type=F32).astype(BF16)
            return carry

        lax.fori_loop(e0, e0 + n, one, 0)

    backs = {0: [], 1: []}

    def back(b, df, dg):
        return remote(p.at[b, 1, SLOT[df, dg]], g.at[b, 1, SLOT[dg, df], pl.ds(0, BODY), :],
                      ys.at[b, SLOT[dg, df]], yr.at[b, SLOT[dg, df]], mate)

    def combine(b, s0, n):
        def one(s, carry):
            r, w = ps[s], ws[s]
            mix = jnp.concatenate(
                [jnp.where(jnp.broadcast_to(r[e:e + 1], (CAP, TOKS)) == cap_i,
                           jnp.broadcast_to(w[e:e + 1], (CAP, TOKS)), 0.0) for e in range(HELD)], axis=0)
            mix = jnp.transpose(mix).astype(BF16)
            for j in range(8):
                k, c = (j // 4 + core) % 2, (j % 4) * 2
                res = jnp.concatenate([xb[e, rows_of(s), pl.ds(j * 256, 256)] for e in range(HELD)], axis=0)
                part = jnp.dot(mix, res, preferred_element_type=F32).astype(BF16)
                p[b, k, s, pl.ds(c * 128, 128), :] = part[:, :128]
                p[b, k, s, pl.ds(c * 128 + 128, 128), :] = part[:, 128:]
            return carry

        lax.fori_loop(s0, s0 + n, one, 0)
        if not backs[b]:
            pl.semaphore_wait(free_sem.at[b], 1)
        for s in range(s0, s0 + n):
            copy = back(b, *ORDER[s])
            copy.start()
            backs[b].append(copy)

    def mate_free(b):
        pl.semaphore_signal(free_sem.at[b], inc=1, device_id={"ep": mate}, device_id_type=MESH)

    def ready(b):
        for copy in (*sent[b], *crossed[b]):
            copy.wait_send()
        for n in nbr.values():
            pl.semaphore_signal(ready_sem.at[b], inc=1, device_id={"ep": n}, device_id_type=MESH)

    home_ids, homes = {}, []

    def hop(b, phase, df, kind):
        i = home_ids.setdefault((phase, df, kind), len(home_ids))
        step = 1 if kind in "tp" else -1
        d = {"t": 2, "b": 2, "p": 1, "m": 3}[kind]
        s = SLOT[(df, d) if phase == 1 else (d, 0)]
        a, n = RET[kind if kind in "tb" else "f"]
        land = (df * 3 if phase == 1 else 12) + {"t": 0, "b": 0, "p": 1, "m": 2}[kind]
        return remote(p.at[b, 0, s, pl.ds(a, n), :], g.at[b, 0, land, pl.ds(a, n), :],
                      rs.at[b, i], rr.at[b, i], nbr["g" if phase == 1 else "f", step])

    def home(*key):
        copy = hop(*key)
        copy.start()
        homes.append(copy)

    def total(b, df, dg, lands):
        s = SLOT[df, dg]
        back(b, dg, df).wait_recv()
        for part in ("t", "b"):
            a, n = RET[part]
            terms = [k for k, span in lands if span in ("f", part)]

            def add(i, carry):
                rows = pl.ds(pl.multiple_of(a + i * 128, 128), 128)
                v = p[b, 0, s, rows, :].astype(F32) + g[b, 1, s, rows, :].astype(F32)
                for k in terms:
                    v = v + g[b, 0, k, rows, :].astype(F32)
                p[b, 0, s, rows, :] = v.astype(BF16)
                return carry

            lax.fori_loop(0, n // 128, add, 0)

    def far(b, df):
        total(b, df, 2, [])
        home(b, 1, df, "t")
        home(b, 1, df, "b")

    def near(b, df):
        hop(b, 1, df, "t").wait_recv()
        total(b, df, 1, [(df * 3, "t")])
        home(b, 1, df, "p")
        hop(b, 1, df, "b").wait_recv()
        total(b, df, 3, [(df * 3, "b")])
        home(b, 1, df, "m")

    def column(b, df):
        hop(b, 1, df, "p").wait_recv()
        hop(b, 1, df, "m").wait_recv()
        lands = [(df * 3 + 1, "f"), (df * 3 + 2, "f")]
        kind = {1: "t", 3: "b"}.get(df)
        if kind:
            hop(b, 2, 2, kind).wait_recv()
            lands.append((12, kind))
        if df == 0:
            hop(b, 2, 1, "p").wait_recv()
            hop(b, 2, 3, "m").wait_recv()
            lands += [(13, "f"), (14, "f")]
        total(b, df, 0, lands)
        if df == 2:
            home(b, 2, 2, "t")
            home(b, 2, 2, "b")
        elif df:
            home(b, 2, df, "p" if df == 1 else "m")

    def store(src, half, i):
        return [pltpu.make_async_copy(
            src.at[pl.ds(c * 128, 128), :],
            out_hbm.at[:, pl.ds(pl.multiple_of(half * HALF + c * 128, 128), 128)], o_sem.at[i * 8 + c]) for c in range(8)]

    handover = remote(p.at[other, 0, 0], fin, fs, fr, mate)

    def finish(b):
        column(b, 0)

        @pl.when(core == b)
        def _():
            for c in store(p.at[b, 0, 0], core, 0):
                c.start()

        @pl.when(core != b)
        def _():
            handover.start()

    ws[...] = jnp.zeros_like(ws)
    for c in halves:
        c.wait_recv()
    first_ring(0)
    for c in sent[0]:
        c.wait_send()
    sent[0].clear()
    second_ring(0, 0)
    arrive(0, 1, 0)
    arrive(0, 3, 0)
    first_ring(1)
    arrive(0, 0, 1)
    arrive(0, 0, 3)
    arrive(0, 2, 0)
    route(0, 0, 5)
    arrive(0, 1, 1)
    arrive(0, 1, 3)
    arrive(0, 3, 1)
    arrive(0, 3, 3)
    arrive(0, 0, 2)
    route(0, 5, 4)
    arrive(0, 2, 1)
    arrive(0, 2, 3)
    second_ring(1, 0)
    arrive(1, 1, 0)
    arrive(1, 3, 0)
    route(0, 9, 2)
    arrive(0, 1, 2)
    arrive(0, 3, 2)
    arrive(0, 2, 2)
    route(0, 11, 5)
    for c in halves:
        c.wait_send()
    mate_free(0)
    for c in loads:
        c.wait()
    expert(0, 1)
    arrive(1, 0, 1)
    arrive(1, 0, 3)
    arrive(1, 2, 0)
    expert(1, 1)
    ready(0)
    arrive(1, 1, 1)
    arrive(1, 1, 3)
    expert(2, 1)
    arrive(1, 3, 1)
    arrive(1, 3, 3)
    arrive(1, 0, 2)
    expert(3, 1)
    combine(0, 9, 7)
    arrive(1, 2, 1)
    arrive(1, 2, 3)
    combine(0, 0, 4)
    pl.semaphore_wait(ready_sem.at[0], 4)
    for df in (2, 1, 3, 0):
        far(0, df)
    combine(0, 4, 5)
    arrive(1, 1, 2)
    arrive(1, 3, 2)
    arrive(1, 2, 2)
    route(1, 0, 9)
    near(0, 2)
    route(1, 9, 7)
    mate_free(1)
    near(0, 1)
    near(0, 3)
    near(0, 0)
    expert(0, 2)
    ready(1)
    column(0, 2)
    expert(2, 2)
    column(0, 1)
    column(0, 3)
    combine(1, 9, 7)
    combine(1, 0, 4)
    pl.semaphore_wait(ready_sem.at[1], 4)
    for df in (2, 1, 3, 0):
        far(1, df)
    combine(1, 4, 5)
    finish(0)
    for df in (2, 1, 3):
        near(1, df)
    column(1, 2)
    near(1, 0)
    column(1, 1)
    column(1, 3)
    finish(1)
    handover.wait_recv()
    rest = store(fin, other, 1)
    for c in rest:
        c.start()
    for copy in (*backs[0], *backs[1], *homes):
        copy.wait_send()
    handover.wait_send()
    for c in (*store(p.at[core, 0, 0], core, 0), *rest):
        c.wait()


def body(tokens, experts, gates, w_gate, w_up, w_down):
    chosen = jnp.pad(experts.astype(BF16).T, ((0, META - experts.shape[1]), (0, 0)), constant_values=-1)
    gate = jnp.pad(gates.T, ((0, META - gates.shape[1]), (0, 0)))
    meta = jnp.stack([chosen, gate])
    dma, any_spec = pltpu.SemaphoreType.DMA, pl.BlockSpec(memory_space=pl.ANY)
    vmem = pl.BlockSpec(memory_space=pltpu.VMEM)
    return pl.pallas_call(
        kernel,
        out_shape=jax.ShapeDtypeStruct((TOKS, WIDTH), BF16),
        in_specs=[any_spec, vmem, any_spec, any_spec, any_spec],
        out_specs=any_spec,
        scratch_shapes=[
            pltpu.VMEM((2, 2, CHIPS, ROWS, 128), BF16),
            pltpu.VMEM((2, 2, CHIPS, BODY, 128), BF16),
            pltpu.VMEM((HELD, WIDTH, HIDDEN), BF16),
            pltpu.VMEM((HELD, WIDTH, HIDDEN), BF16),
            pltpu.VMEM((HELD, WIDTH, HIDDEN), BF16),
            pltpu.VMEM((HELD, CHIPS * CAP, WIDTH), BF16),
            pltpu.VMEM((CHIPS, 8, TOKS), F32),
            pltpu.VMEM((CHIPS, 8, TOKS), F32),
            pltpu.VMEM((BODY, 128), BF16),
            dma((18,)), dma((12,)), dma((2,)), dma((2,)),
            dma((2, 20)), dma((2, 20)), dma((2, 16)), dma((2, 16)), dma((2, 16)), dma((2, 16)),
            dma((2, 20)), dma((2, 20)), dma, dma, dma((16,)),
            pltpu.SemaphoreType.REGULAR((2,)), pltpu.SemaphoreType.REGULAR((2,)),
        ],
        compiler_params=pltpu.CompilerParams(
            collective_id=0, has_side_effects=True, vmem_limit_bytes=67043328),
    )(tokens, meta, w_gate, w_up, w_down)


def solution(mesh):
    in_specs = (
        P(("rep", "ep"), None),
        P(("rep", "ep"), None),
        P(("rep", "ep"), None),
        P("ep", None, None),
        P("ep", None, None),
        P("ep", None, None),
    )
    out_specs = P(("rep", "ep"), None)
    return jax.shard_map(body, mesh=mesh, in_specs=in_specs, out_specs=out_specs, check_vma=False)
```

```python
import jax
import jax.numpy as jnp
from jax import lax
from jax.experimental import pallas as pl
from jax.experimental.pallas import tpu as pltpu
from jax.sharding import PartitionSpec as P

MESH = pl.DeviceIdType.MESH
F32, BF16 = jnp.float32, jnp.bfloat16
SIDE = 4
WIDTH, HIDDEN, TOKS, CAP, HELD = 2048, 512, 128, 16, 4
HALF = WIDTH // 2
BODY, META = 1024, 16
ROWS = BODY + META
SPANS = {"f": (0, ROWS), "t": (0, 528), "b": (528, 512)}
RET = {"f": (0, BODY), "t": (0, 512), "b": (512, 512)}
ORDER = [(0, 0), (1, 0), (3, 0), (0, 1), (0, 3), (1, 1), (1, 3), (3, 1),
         (3, 3), (2, 0), (0, 2), (2, 1), (2, 3), (1, 2), (3, 2), (2, 2)]
SLOT = {d: i for i, d in enumerate(ORDER)}
CHIPS = len(ORDER)


def kernel(tok_hbm, chosen_hbm, gates_hbm, wg_hbm, wu_hbm, wd_hbm, out_hbm,
           g, p, wg, wu, wd, xb, ws, ps, fin,
           ids_v, gates_v, rows_v, own_sem, w_sem, os_, or_, ds, dr, xs, xr, ys, yr, rs, rr, fs, fr, o_sem, free_sem, ready_sem):
    me = lax.axis_index("ep")
    core, x, y = me % 2, (me // 2) % SIDE, me // (2 * SIDE)
    other = 1 - core

    def at(cx, cy, c):
        return (cy * SIDE + cx) * 2 + c

    def pick(along_x, along_y):
        return other * along_x + core * along_y

    xp, xm = at((x + 1) % SIDE, y, core), at((x + SIDE - 1) % SIDE, y, core)
    yp, ym = at(x, (y + 1) % SIDE, core), at(x, (y + SIDE - 1) % SIDE, core)
    nbr = {("f", 1): pick(xp, yp), ("f", -1): pick(xm, ym), ("g", 1): pick(yp, xp), ("g", -1): pick(ym, xm)}
    mate = at(x, y, other)

    def remote(src, dst, send, recv, n):
        return pltpu.make_async_remote_copy(
            src_ref=src, dst_ref=dst, send_sem=send, recv_sem=recv, device_id={"ep": n}, device_id_type=MESH)

    own = []
    for k, half in ((0, core), (1, other)):
        for c in range(8):
            own.append(pltpu.make_async_copy(
                tok_hbm.at[:, pl.ds(pl.multiple_of(half * HALF + c * 128, 128), 128)],
                g.at[core, k, 0, pl.ds(c * 128, 128), :], own_sem.at[k * 9 + c]))
    routing = [pltpu.make_async_copy(chosen_hbm, ids_v, own_sem.at[8]), pltpu.make_async_copy(gates_hbm, gates_v, own_sem.at[17])]
    for c in (*routing, *own):
        c.start()
    loads = []
    for e in range(HELD):
        for i, (src, dst) in enumerate(((wg_hbm, wg), (wu_hbm, wu), (wd_hbm, wd))):
            loads.append(pltpu.make_async_copy(src.at[e], dst.at[e], w_sem.at[e * 3 + i]))
    barrier = pltpu.get_barrier_semaphore()
    for n in (*nbr.values(), mate):
        pl.semaphore_signal(barrier, inc=1, device_id={"ep": n}, device_id_type=MESH)
    ws[...] = jnp.zeros_like(ws)
    topk = ids_v.shape[0]
    rows_v[0] = jnp.full((META, TOKS), -1.0, F32)
    rows_v[1] = jnp.zeros((META, TOKS), F32)
    for c in routing:
        c.wait()
    rows_v[0, pl.ds(0, topk), :] = ids_v[...].astype(F32)
    rows_v[1, pl.ds(0, topk), :] = gates_v[...].astype(F32)
    g[core, core, 0, pl.ds(BODY, META), :] = rows_v[0].astype(BF16)
    g[core, other, 0, pl.ds(BODY, META), :] = rows_v[1].astype(BF16)
    pl.semaphore_wait(barrier, 5)
    for c in own:
        c.wait()
    halves = [remote(g.at[core, 1 - k, 0], g.at[core, k, 0], os_.at[k], or_.at[k], mate) for k in range(2)]
    for c in halves:
        c.start()

    out_ids, sent, crossed = {}, {0: [], 1: []}, {0: [], 1: []}

    def leg(b, df, dg, part):
        i = out_ids.setdefault((df, dg, part), len(out_ids))
        axis, d = ("f", df) if dg == 0 else ("g", dg)
        step = 1 if d == 3 or (d == 2 and part == "t") else -1
        prev = (d + step) % SIDE
        s = SLOT[(prev, 0) if dg == 0 else (df, prev)]
        a, n = SPANS[part]
        return remote(g.at[b, 0, s, pl.ds(a, n), :], g.at[b, 0, SLOT[df, dg], pl.ds(a, n), :],
                      ds.at[b, i], dr.at[b, i], nbr[axis, step])

    def go(b, *key):
        copy = leg(b, *key)
        copy.start()
        sent[b].append(copy)

    def share(b, df, dg):
        return remote(g.at[b, 0, SLOT[df, dg]], g.at[b, 1, SLOT[dg, df]],
                      xs.at[b, SLOT[dg, df]], xr.at[b, SLOT[dg, df]], mate)

    def second_ring(b, df):
        go(b, df, 3, "f")
        go(b, df, 1, "f")

    def first_ring(b):
        go(b, 3, 0, "t")
        go(b, 1, 0, "b")
        go(b, 3, 0, "b")
        go(b, 1, 0, "t")

    def arrive(b, df, dg):
        if dg == 0:
            for part in ("b", "t") if df == 1 else ("t", "b"):
                leg(b, df, 0, part).wait_recv()
                if (df, part) in ((3, "t"), (1, "b")):
                    go(b, 2, 0, part)
            second_ring(b, df)
        else:
            for part in ("t", "b") if dg == 2 else ("f",):
                leg(b, df, dg, part).wait_recv()
            if dg != 2:
                go(b, df, 2, "t" if dg == 3 else "b")
        copy = share(b, df, dg)
        copy.start()
        crossed[b].append(copy)

    row_i = lax.broadcasted_iota(jnp.int32, (TOKS, TOKS), 0)
    col_i = lax.broadcasted_iota(jnp.int32, (TOKS, TOKS), 1)
    before = (row_i < col_i).astype(F32).astype(BF16)
    cap_i = lax.broadcasted_iota(jnp.int32, (CAP, TOKS), 0).astype(F32)

    def rows_of(s):
        return pl.ds(pl.multiple_of(s * CAP, CAP), CAP)

    def route(b, s0, n):
        for s in range(s0, s0 + n):
            if s > 0:
                df, dg = ORDER[s]
                share(b, dg, df).wait_recv()

        def one(s, carry):
            chosen = g[b, core, s, pl.ds(BODY, META), :].astype(F32)
            gate = g[b, other, s, pl.ds(BODY, META), :].astype(F32)
            for e in range(HELD):
                mine = (me * HELD + e).astype(F32)
                ws[s, pl.ds(e, 1), :] = jnp.sum(jnp.where(chosen == mine, gate, 0.0), axis=0, keepdims=True)
            w = ws[s]
            rank = jnp.dot((w > 0.0).astype(F32).astype(BF16), before, preferred_element_type=F32)
            r = jnp.where(w > 0.0, rank, -1.0)
            ps[s] = r
            spread = jnp.concatenate(
                [jnp.where(jnp.broadcast_to(r[e:e + 1], (CAP, TOKS)) == cap_i, 1.0, 0.0) for e in range(HELD)],
                axis=0).astype(BF16)
            for j in range(8):
                k, c = (j // 4 + core) % 2, (j % 4) * 2
                pair = jnp.concatenate(
                    [g[b, k, s, pl.ds(c * 128, 128), :], g[b, k, s, pl.ds(c * 128 + 128, 128), :]], axis=1)
                picked = jnp.dot(spread, pair, preferred_element_type=F32).astype(BF16)
                for e in range(HELD):
                    xb[e, rows_of(s), pl.ds(j * 256, 256)] = picked[e * CAP:(e + 1) * CAP]
            return carry

        lax.fori_loop(s0, s0 + n, one, 0)

    def expert(e0, n):
        def one(e, carry):
            rows = xb[e]
            gate_act = jnp.dot(rows, wg[e], preferred_element_type=F32)
            up_act = jnp.dot(rows, wu[e], preferred_element_type=F32)
            hidden = (gate_act / (1.0 + jnp.exp(-gate_act)) * up_act).astype(BF16)
            for j in range(4):
                xb[e, :, pl.ds(j * 512, 512)] = lax.dot_general(
                    hidden, wd[e, pl.ds(j * 512, 512), :], (((1,), (1,)), ((), ())),
                    preferred_element_type=F32).astype(BF16)
            return carry

        lax.fori_loop(e0, e0 + n, one, 0)

    backs = {0: [], 1: []}

    def back(b, df, dg):
        return remote(p.at[b, 1, SLOT[df, dg]], g.at[b, 1, SLOT[dg, df], pl.ds(0, BODY), :],
                      ys.at[b, SLOT[dg, df]], yr.at[b, SLOT[dg, df]], mate)

    def combine(b, s0, n):
        def one(s, carry):
            r, w = ps[s], ws[s]
            mix = jnp.concatenate(
                [jnp.where(jnp.broadcast_to(r[e:e + 1], (CAP, TOKS)) == cap_i,
                           jnp.broadcast_to(w[e:e + 1], (CAP, TOKS)), 0.0) for e in range(HELD)], axis=0)
            mix = jnp.transpose(mix).astype(BF16)
            for j in range(8):
                k, c = (j // 4 + core) % 2, (j % 4) * 2
                res = jnp.concatenate([xb[e, rows_of(s), pl.ds(j * 256, 256)] for e in range(HELD)], axis=0)
                part = jnp.dot(mix, res, preferred_element_type=F32).astype(BF16)
                p[b, k, s, pl.ds(c * 128, 128), :] = part[:, :128]
                p[b, k, s, pl.ds(c * 128 + 128, 128), :] = part[:, 128:]
            return carry

        lax.fori_loop(s0, s0 + n, one, 0)
        if not backs[b]:
            pl.semaphore_wait(free_sem.at[b], 1)
        for s in range(s0, s0 + n):
            copy = back(b, *ORDER[s])
            copy.start()
            backs[b].append(copy)

    def mate_free(b):
        pl.semaphore_signal(free_sem.at[b], inc=1, device_id={"ep": mate}, device_id_type=MESH)

    def ready(b):
        for copy in (*sent[b], *crossed[b]):
            copy.wait_send()
        for n in nbr.values():
            pl.semaphore_signal(ready_sem.at[b], inc=1, device_id={"ep": n}, device_id_type=MESH)

    home_ids, homes = {}, []

    def hop(b, phase, df, kind):
        i = home_ids.setdefault((phase, df, kind), len(home_ids))
        step = 1 if kind in "tp" else -1
        d = {"t": 2, "b": 2, "p": 1, "m": 3}[kind]
        s = SLOT[(df, d) if phase == 1 else (d, 0)]
        a, n = RET[kind if kind in "tb" else "f"]
        land = (df * 3 if phase == 1 else 12) + {"t": 0, "b": 0, "p": 1, "m": 2}[kind]
        return remote(p.at[b, 0, s, pl.ds(a, n), :], g.at[b, 0, land, pl.ds(a, n), :],
                      rs.at[b, i], rr.at[b, i], nbr["g" if phase == 1 else "f", step])

    def home(*key):
        copy = hop(*key)
        copy.start()
        homes.append(copy)

    def total(b, df, dg, lands):
        s = SLOT[df, dg]
        back(b, dg, df).wait_recv()
        for part in ("t", "b"):
            a, n = RET[part]
            terms = [k for k, span in lands if span in ("f", part)]

            def add(i, carry):
                rows = pl.ds(pl.multiple_of(a + i * 128, 128), 128)
                v = p[b, 0, s, rows, :].astype(F32) + g[b, 1, s, rows, :].astype(F32)
                for k in terms:
                    v = v + g[b, 0, k, rows, :].astype(F32)
                p[b, 0, s, rows, :] = v.astype(BF16)
                return carry

            lax.fori_loop(0, n // 128, add, 0)

    def far(b, df):
        total(b, df, 2, [])
        home(b, 1, df, "t")
        home(b, 1, df, "b")

    def near(b, df):
        hop(b, 1, df, "t").wait_recv()
        total(b, df, 1, [(df * 3, "t")])
        home(b, 1, df, "p")
        hop(b, 1, df, "b").wait_recv()
        total(b, df, 3, [(df * 3, "b")])
        home(b, 1, df, "m")

    def column(b, df):
        hop(b, 1, df, "p").wait_recv()
        hop(b, 1, df, "m").wait_recv()
        lands = [(df * 3 + 1, "f"), (df * 3 + 2, "f")]
        kind = {1: "t", 3: "b"}.get(df)
        if kind:
            hop(b, 2, 2, kind).wait_recv()
            lands.append((12, kind))
        if df == 0:
            hop(b, 2, 1, "p").wait_recv()
            hop(b, 2, 3, "m").wait_recv()
            lands += [(13, "f"), (14, "f")]
        total(b, df, 0, lands)
        if df == 2:
            home(b, 2, 2, "t")
            home(b, 2, 2, "b")
        elif df:
            home(b, 2, df, "p" if df == 1 else "m")

    def store(src, half, i):
        return [pltpu.make_async_copy(
            src.at[pl.ds(c * 128, 128), :],
            out_hbm.at[:, pl.ds(pl.multiple_of(half * HALF + c * 128, 128), 128)], o_sem.at[i * 8 + c]) for c in range(8)]

    handover = remote(p.at[other, 0, 0], fin, fs, fr, mate)

    def finish(b):
        column(b, 0)

        @pl.when(core == b)
        def _():
            for c in store(p.at[b, 0, 0], core, 0):
                c.start()

        @pl.when(core != b)
        def _():
            handover.start()

    for c in halves:
        c.wait_recv()
    first_ring(0)
    for c in sent[0][:2]:
        c.wait_send()
    del sent[0][:2]
    second_ring(0, 0)
    for c in loads:
        c.start()
    arrive(0, 1, 0)
    arrive(0, 3, 0)
    first_ring(1)
    arrive(0, 0, 1)
    arrive(0, 0, 3)
    arrive(0, 2, 0)
    route(0, 0, 5)
    arrive(0, 1, 1)
    arrive(0, 1, 3)
    arrive(0, 3, 1)
    arrive(0, 3, 3)
    arrive(0, 0, 2)
    route(0, 5, 4)
    arrive(0, 2, 1)
    arrive(0, 2, 3)
    second_ring(1, 0)
    arrive(1, 1, 0)
    arrive(1, 3, 0)
    route(0, 9, 2)
    arrive(0, 1, 2)
    arrive(0, 3, 2)
    arrive(0, 2, 2)
    route(0, 11, 5)
    for c in halves:
        c.wait_send()
    mate_free(0)
    for c in loads:
        c.wait()
    expert(0, 1)
    arrive(1, 0, 1)
    arrive(1, 0, 3)
    arrive(1, 2, 0)
    expert(1, 1)
    ready(0)
    arrive(1, 1, 1)
    arrive(1, 1, 3)
    expert(2, 1)
    arrive(1, 3, 1)
    arrive(1, 3, 3)
    arrive(1, 0, 2)
    expert(3, 1)
    combine(0, 11, 5)
    combine(0, 9, 2)
    arrive(1, 2, 1)
    arrive(1, 2, 3)
    combine(0, 5, 4)
    pl.semaphore_wait(ready_sem.at[0], 4)
    far(0, 2)
    far(0, 1)
    far(0, 3)
    combine(0, 0, 5)
    arrive(1, 1, 2)
    arrive(1, 3, 2)
    arrive(1, 2, 2)
    far(0, 0)
    route(1, 0, 5)
    near(0, 2)
    route(1, 5, 4)
    near(0, 1)
    near(0, 3)
    route(1, 9, 7)
    mate_free(1)
    near(0, 0)
    expert(0, 1)
    ready(1)
    expert(1, 1)
    column(0, 2)
    expert(2, 2)
    column(0, 1)
    column(0, 3)
    combine(1, 11, 5)
    combine(1, 9, 2)
    pl.semaphore_wait(ready_sem.at[1], 4)
    far(1, 2)
    far(1, 1)
    far(1, 3)
    far(1, 0)
    combine(1, 5, 4)
    near(1, 2)
    combine(1, 0, 5)
    near(1, 1)
    near(1, 3)
    column(1, 2)
    near(1, 0)
    finish(0)
    column(1, 1)
    column(1, 3)
    finish(1)
    handover.wait_recv()
    rest = store(fin, other, 1)
    for c in rest:
        c.start()
    for copy in (*backs[0], *backs[1], *homes):
        copy.wait_send()
    handover.wait_send()
    for c in (*store(p.at[core, 0, 0], core, 0), *rest):
        c.wait()


def body(tokens, experts, gates, w_gate, w_up, w_down):
    dma, any_spec = pltpu.SemaphoreType.DMA, pl.BlockSpec(memory_space=pl.ANY)
    return pl.pallas_call(
        kernel,
        out_shape=jax.ShapeDtypeStruct((TOKS, WIDTH), BF16),
        in_specs=[any_spec] * 6,
        out_specs=any_spec,
        scratch_shapes=[
            pltpu.VMEM((2, 2, CHIPS, ROWS, 128), BF16),
            pltpu.VMEM((2, 2, CHIPS, BODY, 128), BF16),
            pltpu.VMEM((HELD, WIDTH, HIDDEN), BF16),
            pltpu.VMEM((HELD, WIDTH, HIDDEN), BF16),
            pltpu.VMEM((HELD, WIDTH, HIDDEN), BF16),
            pltpu.VMEM((HELD, CHIPS * CAP, WIDTH), BF16),
            pltpu.VMEM((CHIPS, 8, TOKS), F32),
            pltpu.VMEM((CHIPS, 8, TOKS), F32),
            pltpu.VMEM((BODY, 128), BF16),
            pltpu.VMEM((experts.shape[1], TOKS), jnp.int32),
            pltpu.VMEM((gates.shape[1], TOKS), BF16),
            pltpu.VMEM((2, META, TOKS), F32),
            dma((18,)), dma((12,)), dma((2,)), dma((2,)),
            dma((2, 22)), dma((2, 22)), dma((2, 16)), dma((2, 16)), dma((2, 16)), dma((2, 16)),
            dma((2, 20)), dma((2, 20)), dma, dma, dma((16,)),
            pltpu.SemaphoreType.REGULAR((2,)), pltpu.SemaphoreType.REGULAR((2,)),
        ],
        compiler_params=pltpu.CompilerParams(
            collective_id=0, has_side_effects=True, vmem_limit_bytes=67043328),
    )(tokens, experts.T, gates.T, w_gate, w_up, w_down)


def solution(mesh):
    in_specs = (
        P(("rep", "ep"), None),
        P(("rep", "ep"), None),
        P(("rep", "ep"), None),
        P("ep", None, None),
        P("ep", None, None),
        P("ep", None, None),
    )
    out_specs = P(("rep", "ep"), None)
    return jax.shard_map(body, mesh=mesh, in_specs=in_specs, out_specs=out_specs, check_vma=False)
```

```python
import jax
import jax.numpy as jnp
from jax import lax
from jax.experimental import pallas as pl
from jax.experimental.pallas import tpu as pltpu
from jax.sharding import PartitionSpec as P

MESH = pl.DeviceIdType.MESH
F32, BF16 = jnp.float32, jnp.bfloat16
SIDE = 4
WIDTH, HIDDEN, TOKS, CAP, HELD = 2048, 512, 128, 16, 4
HALF = WIDTH // 2
BODY, META = 1024, 16
ROWS = BODY + META
SPANS = {"f": (0, ROWS), "t": (0, 528), "b": (528, 512)}
RET = {"f": (0, BODY), "t": (0, 512), "b": (512, 512)}
ORDER = [(0, 0), (1, 0), (3, 0), (0, 1), (0, 3), (1, 1), (1, 3), (3, 1),
         (3, 3), (2, 0), (0, 2), (2, 1), (2, 3), (1, 2), (3, 2), (2, 2)]
SLOT = {d: i for i, d in enumerate(ORDER)}
CHIPS = len(ORDER)


def kernel(tok_hbm, chosen_hbm, gates_hbm, wg_hbm, wu_hbm, wd_hbm, out_hbm,
           g, p, wg, wu, wd, xb, ws, ps, fin,
           ids_v, gates_v, rows_v, own_sem, w_sem, os_, or_, ds, dr, xs, xr, ys, yr, rs, rr, fs, fr, o_sem, free_sem, ready_sem):
    me = lax.axis_index("ep")
    core, x, y = me % 2, (me // 2) % SIDE, me // (2 * SIDE)
    other = 1 - core

    def at(cx, cy, c):
        return (cy * SIDE + cx) * 2 + c

    def pick(along_x, along_y):
        return other * along_x + core * along_y

    xp, xm = at((x + 1) % SIDE, y, core), at((x + SIDE - 1) % SIDE, y, core)
    yp, ym = at(x, (y + 1) % SIDE, core), at(x, (y + SIDE - 1) % SIDE, core)
    nbr = {("f", 1): pick(xp, yp), ("f", -1): pick(xm, ym), ("g", 1): pick(yp, xp), ("g", -1): pick(ym, xm)}
    mate = at(x, y, other)

    def remote(src, dst, send, recv, n):
        return pltpu.make_async_remote_copy(
            src_ref=src, dst_ref=dst, send_sem=send, recv_sem=recv, device_id={"ep": n}, device_id_type=MESH)

    own = []
    for k, half in ((0, core), (1, other)):
        for c in range(8):
            own.append(pltpu.make_async_copy(
                tok_hbm.at[:, pl.ds(pl.multiple_of(half * HALF + c * 128, 128), 128)],
                g.at[core, k, 0, pl.ds(c * 128, 128), :], own_sem.at[k * 9 + c]))
    routing = [pltpu.make_async_copy(chosen_hbm, ids_v, own_sem.at[8]), pltpu.make_async_copy(gates_hbm, gates_v, own_sem.at[17])]
    for c in (*routing, *own):
        c.start()
    loads = []
    for e in range(HELD):
        for i, (src, dst) in enumerate(((wg_hbm, wg), (wu_hbm, wu), (wd_hbm, wd))):
            loads.append(pltpu.make_async_copy(src.at[e], dst.at[e], w_sem.at[e * 3 + i]))
    barrier = pltpu.get_barrier_semaphore()
    for n in (*nbr.values(), mate):
        pl.semaphore_signal(barrier, inc=1, device_id={"ep": n}, device_id_type=MESH)
    ws[...] = jnp.zeros_like(ws)
    topk = ids_v.shape[0]
    rows_v[0] = jnp.full((META, TOKS), -1.0, F32)
    rows_v[1] = jnp.zeros((META, TOKS), F32)
    for c in routing:
        c.wait()
    rows_v[0, pl.ds(0, topk), :] = ids_v[...].astype(F32)
    rows_v[1, pl.ds(0, topk), :] = gates_v[...].astype(F32)
    g[core, core, 0, pl.ds(BODY, META), :] = rows_v[0].astype(BF16)
    g[core, other, 0, pl.ds(BODY, META), :] = rows_v[1].astype(BF16)
    pl.semaphore_wait(barrier, 5)
    for c in own:
        c.wait()
    halves = [remote(g.at[core, 1 - k, 0], g.at[core, k, 0], os_.at[k], or_.at[k], mate) for k in range(2)]
    for c in halves:
        c.start()

    out_ids, sent, crossed = {}, {0: [], 1: []}, {0: [], 1: []}

    def leg(b, df, dg, part):
        i = out_ids.setdefault((df, dg, part), len(out_ids))
        axis, d = ("f", df) if dg == 0 else ("g", dg)
        step = 1 if d == 3 or (d == 2 and part == "t") else -1
        prev = (d + step) % SIDE
        s = SLOT[(prev, 0) if dg == 0 else (df, prev)]
        a, n = SPANS[part]
        return remote(g.at[b, 0, s, pl.ds(a, n), :], g.at[b, 0, SLOT[df, dg], pl.ds(a, n), :],
                      ds.at[b, i], dr.at[b, i], nbr[axis, step])

    def go(b, *key):
        copy = leg(b, *key)
        copy.start()
        sent[b].append(copy)

    def share(b, df, dg):
        return remote(g.at[b, 0, SLOT[df, dg]], g.at[b, 1, SLOT[dg, df]],
                      xs.at[b, SLOT[dg, df]], xr.at[b, SLOT[dg, df]], mate)

    def second_ring(b, df):
        go(b, df, 3, "f")
        go(b, df, 1, "f")

    def first_ring(b):
        go(b, 3, 0, "t")
        go(b, 1, 0, "b")
        go(b, 3, 0, "b")
        go(b, 1, 0, "t")

    def arrive(b, df, dg):
        if dg == 0:
            for part in ("b", "t") if df == 1 else ("t", "b"):
                leg(b, df, 0, part).wait_recv()
                if (df, part) in ((3, "t"), (1, "b")):
                    go(b, 2, 0, part)
            second_ring(b, df)
        else:
            for part in ("t", "b") if dg == 2 else ("f",):
                leg(b, df, dg, part).wait_recv()
            if dg != 2:
                go(b, df, 2, "t" if dg == 3 else "b")
        copy = share(b, df, dg)
        copy.start()
        crossed[b].append(copy)

    row_i = lax.broadcasted_iota(jnp.int32, (TOKS, TOKS), 0)
    col_i = lax.broadcasted_iota(jnp.int32, (TOKS, TOKS), 1)
    before = (row_i < col_i).astype(F32).astype(BF16)
    cap_i = lax.broadcasted_iota(jnp.int32, (CAP, TOKS), 0).astype(F32)

    def rows_of(s):
        return pl.ds(pl.multiple_of(s * CAP, CAP), CAP)

    def several(one, s0, n):
        at_once = 5 if n % 5 == 0 else 4 if n % 4 == 0 else 3 if n % 3 == 0 else n

        def some(i, carry):
            for j in range(at_once):
                one(s0 + i * at_once + j)
            return carry

        lax.fori_loop(0, n // at_once, some, 0)

    def route(b, s0, n):
        for s in range(s0, s0 + n):
            if s > 0:
                df, dg = ORDER[s]
                share(b, dg, df).wait_recv()

        def weigh(s, carry):
            chosen = g[b, core, s, pl.ds(BODY, META), :].astype(F32)
            gate = g[b, other, s, pl.ds(BODY, META), :].astype(F32)
            for e in range(HELD):
                mine = (me * HELD + e).astype(F32)
                ws[s, pl.ds(e, 1), :] = jnp.sum(jnp.where(chosen == mine, gate, 0.0), axis=0, keepdims=True)
            return carry

        lax.fori_loop(s0, s0 + n, weigh, 0)
        w = ws[pl.ds(s0, n)].reshape(n * 8, TOKS)
        rank = jnp.dot((w > 0.0).astype(F32).astype(BF16), before, preferred_element_type=F32)
        ps[pl.ds(s0, n)] = jnp.where(w > 0.0, rank, -1.0).reshape(n, 8, TOKS)

        def one(s):
            r = ps[s]
            spread = jnp.concatenate(
                [jnp.where(jnp.broadcast_to(r[e:e + 1], (CAP, TOKS)) == cap_i, 1.0, 0.0) for e in range(HELD)],
                axis=0).astype(BF16)
            for j in range(8):
                k, c = (j // 4 + core) % 2, (j % 4) * 2
                pair = jnp.concatenate(
                    [g[b, k, s, pl.ds(c * 128, 128), :], g[b, k, s, pl.ds(c * 128 + 128, 128), :]], axis=1)
                picked = jnp.dot(spread, pair, preferred_element_type=F32).astype(BF16)
                for e in range(HELD):
                    xb[e, rows_of(s), pl.ds(j * 256, 256)] = picked[e * CAP:(e + 1) * CAP]

        several(one, s0, n)

    def expert(e0, n):
        def one(e, carry):
            rows = xb[e]
            gate_act = jnp.dot(rows, wg[e], preferred_element_type=F32)
            up_act = jnp.dot(rows, wu[e], preferred_element_type=F32)
            hidden = (gate_act / (1.0 + jnp.exp(-gate_act)) * up_act).astype(BF16)
            for j in range(4):
                xb[e, :, pl.ds(j * 512, 512)] = lax.dot_general(
                    hidden, wd[e, pl.ds(j * 512, 512), :], (((1,), (1,)), ((), ())),
                    preferred_element_type=F32).astype(BF16)
            return carry

        lax.fori_loop(e0, e0 + n, one, 0)

    backs = {0: [], 1: []}

    def back(b, df, dg):
        return remote(p.at[b, 1, SLOT[df, dg]], g.at[b, 1, SLOT[dg, df], pl.ds(0, BODY), :],
                      ys.at[b, SLOT[dg, df]], yr.at[b, SLOT[dg, df]], mate)

    def combine(b, s0, n):
        def one(s):
            r, w = ps[s], ws[s]
            mix = jnp.concatenate(
                [jnp.where(jnp.broadcast_to(r[e:e + 1], (CAP, TOKS)) == cap_i,
                           jnp.broadcast_to(w[e:e + 1], (CAP, TOKS)), 0.0) for e in range(HELD)], axis=0)
            mix = jnp.transpose(mix).astype(BF16)
            for j in range(8):
                k, c = (j // 4 + core) % 2, (j % 4) * 2
                res = jnp.concatenate([xb[e, rows_of(s), pl.ds(j * 256, 256)] for e in range(HELD)], axis=0)
                part = jnp.dot(mix, res, preferred_element_type=F32).astype(BF16)
                p[b, k, s, pl.ds(c * 128, 128), :] = part[:, :128]
                p[b, k, s, pl.ds(c * 128 + 128, 128), :] = part[:, 128:]

        several(one, s0, n)
        if not backs[b]:
            pl.semaphore_wait(free_sem.at[b], 1)
        for s in range(s0, s0 + n):
            copy = back(b, *ORDER[s])
            copy.start()
            backs[b].append(copy)

    def mate_free(b):
        pl.semaphore_signal(free_sem.at[b], inc=1, device_id={"ep": mate}, device_id_type=MESH)

    def ready(b):
        for copy in (*sent[b], *crossed[b]):
            copy.wait_send()
        for n in nbr.values():
            pl.semaphore_signal(ready_sem.at[b], inc=1, device_id={"ep": n}, device_id_type=MESH)

    home_ids, homes = {}, []

    def hop(b, phase, df, kind):
        i = home_ids.setdefault((phase, df, kind), len(home_ids))
        step = 1 if kind[0] in "tp" else -1
        d = {"t": 2, "b": 2, "p": 1, "m": 3}[kind[0]]
        s = SLOT[(df, d) if phase == 1 else (d, 0)]
        a, n = RET[kind[-1]]
        land = (df * 3 if phase == 1 else 12) + {"t": 0, "b": 0, "p": 1, "m": 2}[kind[0]]
        return remote(p.at[b, 0, s, pl.ds(a, n), :], g.at[b, 0, land, pl.ds(a, n), :],
                      rs.at[b, i], rr.at[b, i], nbr["g" if phase == 1 else "f", step])

    def home(*key):
        copy = hop(*key)
        copy.start()
        homes.append(copy)

    came = set()

    def total(b, df, dg, lands, parts="tb"):
        s = SLOT[df, dg]
        if (b, s) not in came:
            back(b, dg, df).wait_recv()
            came.add((b, s))
        for part in parts:
            a, n = RET[part]

            def add(i, carry):
                rows = pl.ds(pl.multiple_of(a + i * 128, 128), 128)
                v = p[b, 0, s, rows, :].astype(F32) + g[b, 1, s, rows, :].astype(F32)
                for k in lands:
                    v = v + g[b, 0, k, rows, :].astype(F32)
                p[b, 0, s, rows, :] = v.astype(BF16)
                return carry

            lax.fori_loop(0, n // 128, add, 0)

    def took(b, phase, df, *kinds):
        for kind in kinds:
            hop(b, phase, df, kind).wait_recv()

    def far(b, df):
        total(b, df, 2, [])
        home(b, 1, df, "t")
        home(b, 1, df, "b")

    def free(b, df):
        total(b, df, 1, [], "b")
        home(b, 1, df, "pb")
        total(b, df, 3, [], "t")
        home(b, 1, df, "mt")

    def near(b, df):
        took(b, 1, df, "t")
        total(b, df, 1, [df * 3], "t")
        home(b, 1, df, "pt")
        took(b, 1, df, "b")
        total(b, df, 3, [df * 3], "b")
        home(b, 1, df, "mb")

    def column(b, df, part):
        took(b, 1, df, "p" + part, "m" + part)
        lands = [df * 3 + 1, df * 3 + 2]
        if (df, part) in ((1, "t"), (3, "b")):
            took(b, 2, 2, part)
            lands.append(12)
        if df == 0:
            took(b, 2, 1, "p" + part)
            took(b, 2, 3, "m" + part)
            lands += [13, 14]
        total(b, df, 0, lands, part)
        if df:
            home(b, 2, df, {1: "p", 2: "", 3: "m"}[df] + part)

    def store(src, half, i):
        return [pltpu.make_async_copy(
            src.at[pl.ds(c * 128, 128), :],
            out_hbm.at[:, pl.ds(pl.multiple_of(half * HALF + c * 128, 128), 128)], o_sem.at[i * 8 + c]) for c in range(8)]

    handover = remote(p.at[other, 0, 0], fin, fs, fr, mate)

    def finish(b):
        column(b, 0, "t")
        column(b, 0, "b")

        @pl.when(core == b)
        def _():
            for c in store(p.at[b, 0, 0], core, 0):
                c.start()

        @pl.when(core != b)
        def _():
            handover.start()

    for c in halves:
        c.wait_recv()
    first_ring(0)
    for c in sent[0][:2]:
        c.wait_send()
    del sent[0][:2]
    second_ring(0, 0)
    for c in loads:
        c.start()
    arrive(0, 1, 0)
    arrive(0, 3, 0)
    first_ring(1)
    arrive(0, 0, 1)
    arrive(0, 0, 3)
    arrive(0, 2, 0)
    route(0, 0, 5)
    arrive(0, 1, 1)
    arrive(0, 1, 3)
    arrive(0, 3, 1)
    arrive(0, 3, 3)
    route(0, 5, 4)
    arrive(0, 2, 1)
    arrive(0, 2, 3)
    second_ring(1, 0)
    arrive(1, 1, 0)
    arrive(1, 3, 0)
    arrive(0, 0, 2)
    route(0, 9, 2)
    arrive(0, 1, 2)
    arrive(0, 3, 2)
    arrive(0, 2, 2)
    route(0, 11, 5)
    for c in halves:
        c.wait_send()
    mate_free(0)
    for c in loads:
        c.wait()
    expert(0, 1)
    arrive(1, 0, 1)
    arrive(1, 0, 3)
    arrive(1, 2, 0)
    expert(1, 1)
    ready(0)
    arrive(1, 1, 1)
    arrive(1, 1, 3)
    expert(2, 1)
    arrive(1, 3, 1)
    expert(3, 1)
    arrive(1, 3, 3)
    combine(0, 11, 5)
    combine(0, 9, 2)
    arrive(1, 2, 1)
    combine(0, 5, 4)
    arrive(1, 2, 3)
    arrive(1, 0, 2)
    pl.semaphore_wait(ready_sem.at[0], 4)
    far(0, 2)
    far(0, 1)
    free(0, 2)
    far(0, 3)
    combine(0, 0, 5)
    free(0, 1)
    far(0, 0)
    free(0, 3)
    free(0, 0)
    arrive(1, 1, 2)
    arrive(1, 3, 2)
    arrive(1, 2, 2)
    route(1, 0, 5)
    route(1, 5, 4)
    near(0, 2)
    route(1, 9, 7)
    mate_free(1)
    ready(1)
    expert(0, 2)
    near(0, 1)
    near(0, 3)
    expert(2, 1)
    near(0, 0)
    expert(3, 1)
    column(0, 2, "t")
    column(0, 2, "b")
    combine(1, 11, 5)
    combine(1, 9, 2)
    combine(1, 5, 4)
    pl.semaphore_wait(ready_sem.at[1], 4)
    far(1, 2)
    far(1, 1)
    free(1, 2)
    far(1, 3)
    column(0, 1, "b")
    column(0, 3, "t")
    combine(1, 0, 5)
    free(1, 1)
    near(1, 2)
    column(0, 1, "t")
    column(0, 3, "b")
    far(1, 0)
    free(1, 3)
    near(1, 1)
    near(1, 3)
    column(1, 2, "t")
    column(1, 2, "b")
    free(1, 0)
    near(1, 0)
    finish(0)
    column(1, 1, "b")
    column(1, 3, "t")
    column(1, 1, "t")
    column(1, 3, "b")
    finish(1)
    handover.wait_recv()
    rest = store(fin, other, 1)
    for c in rest:
        c.start()
    for copy in (*backs[0], *backs[1], *homes):
        copy.wait_send()
    handover.wait_send()
    for c in (*store(p.at[core, 0, 0], core, 0), *rest):
        c.wait()


def body(tokens, experts, gates, w_gate, w_up, w_down):
    dma, any_spec = pltpu.SemaphoreType.DMA, pl.BlockSpec(memory_space=pl.ANY)
    return pl.pallas_call(
        kernel,
        out_shape=jax.ShapeDtypeStruct((TOKS, WIDTH), BF16),
        in_specs=[any_spec] * 6,
        out_specs=any_spec,
        scratch_shapes=[
            pltpu.VMEM((2, 2, CHIPS, ROWS, 128), BF16),
            pltpu.VMEM((2, 2, CHIPS, BODY, 128), BF16),
            pltpu.VMEM((HELD, WIDTH, HIDDEN), BF16),
            pltpu.VMEM((HELD, WIDTH, HIDDEN), BF16),
            pltpu.VMEM((HELD, WIDTH, HIDDEN), BF16),
            pltpu.VMEM((HELD, CHIPS * CAP, WIDTH), BF16),
            pltpu.VMEM((CHIPS, 8, TOKS), F32),
            pltpu.VMEM((CHIPS, 8, TOKS), F32),
            pltpu.VMEM((BODY, 128), BF16),
            pltpu.VMEM((experts.shape[1], TOKS), jnp.int32),
            pltpu.VMEM((gates.shape[1], TOKS), BF16),
            pltpu.VMEM((2, META, TOKS), F32),
            dma((18,)), dma((12,)), dma((2,)), dma((2,)),
            dma((2, 22)), dma((2, 22)), dma((2, 16)), dma((2, 16)), dma((2, 16)), dma((2, 16)),
            dma((2, 30)), dma((2, 30)), dma, dma, dma((16,)),
            pltpu.SemaphoreType.REGULAR((2,)), pltpu.SemaphoreType.REGULAR((2,)),
        ],
        compiler_params=pltpu.CompilerParams(
            collective_id=0, has_side_effects=True, vmem_limit_bytes=67043328),
    )(tokens, experts.T, gates.T, w_gate, w_up, w_down)


def solution(mesh):
    in_specs = (
        P(("rep", "ep"), None),
        P(("rep", "ep"), None),
        P(("rep", "ep"), None),
        P("ep", None, None),
        P("ep", None, None),
        P("ep", None, None),
    )
    out_specs = P(("rep", "ep"), None)
    return jax.shard_map(body, mesh=mesh, in_specs=in_specs, out_specs=out_specs, check_vma=False)
```

```python
import jax
import jax.numpy as jnp
from jax import lax
from jax.experimental import pallas as pl
from jax.experimental.pallas import tpu as pltpu
from jax.sharding import PartitionSpec as P

MESH = pl.DeviceIdType.MESH
F32, BF16 = jnp.float32, jnp.bfloat16
SIDE = 4
WIDTH, HIDDEN, TOKS, CAP, HELD = 2048, 512, 128, 16, 4
HALF = WIDTH // 2
BODY, META = 1024, 16
ROWS = BODY + META
SPANS = {"f": (0, ROWS), "t": (0, 528), "b": (528, 512)}
RET = {"f": (0, BODY), "t": (0, 512), "b": (512, 512)}
ORDER = [(0, 0), (1, 0), (3, 0), (0, 1), (0, 3), (1, 1), (1, 3), (3, 1),
         (3, 3), (2, 0), (0, 2), (2, 1), (2, 3), (1, 2), (3, 2), (2, 2)]
SLOT = {d: i for i, d in enumerate(ORDER)}
CHIPS = len(ORDER)


def kernel(tok_hbm, chosen_hbm, gates_hbm, wg_hbm, wu_hbm, wd_hbm, out_ref,
           g, p, wg, wu, wd, xb, ws, ps, fin,
           ids_v, gates_v, rows_v, own_sem, w_sem, os_, or_, es, ds, dr, xs, xr, ys, rs, fs, fr, free_sem, ready_sem):
    me = lax.axis_index("ep")
    core, x, y = me % 2, (me // 2) % SIDE, me // (2 * SIDE)
    other = 1 - core

    def at(cx, cy, c):
        return (cy * SIDE + cx) * 2 + c

    def pick(along_x, along_y):
        return other * along_x + core * along_y

    xp, xm = at((x + 1) % SIDE, y, core), at((x + SIDE - 1) % SIDE, y, core)
    yp, ym = at(x, (y + 1) % SIDE, core), at(x, (y + SIDE - 1) % SIDE, core)
    nbr = {("f", 1): pick(xp, yp), ("f", -1): pick(xm, ym), ("g", 1): pick(yp, xp), ("g", -1): pick(ym, xm)}
    mate = at(x, y, other)

    def remote(src, dst, send, recv, n):
        return pltpu.make_async_remote_copy(
            src_ref=src, dst_ref=dst, send_sem=send, recv_sem=recv, device_id={"ep": n}, device_id_type=MESH)

    own = []
    for k, half in ((0, core), (1, other)):
        for c in range(8):
            own.append(pltpu.make_async_copy(
                tok_hbm.at[:, pl.ds(pl.multiple_of(half * HALF + c * 128, 128), 128)],
                g.at[core, k, 0, pl.ds(c * 128, 128), :], own_sem.at[k * 9 + c]))
    routing = [pltpu.make_async_copy(chosen_hbm, ids_v, own_sem.at[8]), pltpu.make_async_copy(gates_hbm, gates_v, own_sem.at[17])]
    for c in (*routing, *own):
        c.start()
    loads = []
    for i, (src, dst) in enumerate(((wg_hbm, wg), (wu_hbm, wu), (wd_hbm, wd))):
        loads.append(pltpu.make_async_copy(src, dst, w_sem.at[i]))
    barrier = pltpu.get_barrier_semaphore()
    for n in (*nbr.values(), mate):
        pl.semaphore_signal(barrier, inc=1, device_id={"ep": n}, device_id_type=MESH)
    ws[...] = jnp.zeros_like(ws)
    topk = ids_v.shape[0]
    rows_v[0] = jnp.full((META, TOKS), -1.0, F32)
    rows_v[1] = jnp.zeros((META, TOKS), F32)
    for c in routing:
        c.wait()
    rows_v[0, pl.ds(0, topk), :] = ids_v[...].astype(F32)
    rows_v[1, pl.ds(0, topk), :] = gates_v[...].astype(F32)
    g[core, core, 0, pl.ds(BODY, META), :] = rows_v[0].astype(BF16)
    g[core, other, 0, pl.ds(BODY, META), :] = rows_v[1].astype(BF16)
    pl.semaphore_wait(barrier, 5)
    for c in own:
        c.wait()
    halves = [remote(g.at[core, 1 - k, 0], g.at[core, k, 0], os_.at[k], or_.at[k], mate) for k in range(2)]
    for c in halves:
        c.start()

    out_ids, early = {}, {(3, 0, "t"): 0, (1, 0, "b"): 1}

    def leg(b, df, dg, part):
        i = out_ids.setdefault((df, dg, part), len(out_ids))
        axis, d = ("f", df) if dg == 0 else ("g", dg)
        step = 1 if d == 3 or (d == 2 and part == "t") else -1
        prev = (d + step) % SIDE
        s = SLOT[(prev, 0) if dg == 0 else (df, prev)]
        a, n = SPANS[part]
        return remote(g.at[b, 0, s, pl.ds(a, n), :], g.at[b, 0, SLOT[df, dg], pl.ds(a, n), :],
                      es.at[early[df, dg, part]] if b == 0 and (df, dg, part) in early else ds.at[b],
                      dr.at[b, i], nbr[axis, step])

    def go(b, *key):
        leg(b, *key).start()

    def share(b, df, dg):
        return remote(g.at[b, 0, SLOT[df, dg]], g.at[b, 1, SLOT[dg, df]],
                      xs.at[b], xr.at[b, SLOT[dg, df]], mate)

    def second_ring(b, df):
        go(b, df, 3, "f")
        go(b, df, 1, "f")

    def first_ring(b, parts=2):
        if parts != 1:
            go(b, 3, 0, "t")
            go(b, 1, 0, "b")
        if parts != 0:
            go(b, 3, 0, "b")
            go(b, 1, 0, "t")

    def arrive(b, df, dg):
        if dg == 0:
            for part in ("b", "t") if df == 1 else ("t", "b"):
                leg(b, df, 0, part).wait_recv()
                if (df, part) in ((3, "t"), (1, "b")):
                    go(b, 2, 0, part)
            second_ring(b, df)
        else:
            for part in ("t", "b") if dg == 2 else ("f",):
                leg(b, df, dg, part).wait_recv()
            if dg != 2:
                go(b, df, 2, "t" if dg == 3 else "b")
        share(b, df, dg).start()

    row_i = lax.broadcasted_iota(jnp.int32, (TOKS, TOKS), 0)
    col_i = lax.broadcasted_iota(jnp.int32, (TOKS, TOKS), 1)
    before = (row_i < col_i).astype(F32).astype(BF16)
    cap_i = lax.broadcasted_iota(jnp.int32, (CAP, TOKS), 0).astype(F32)

    def rows_of(s):
        return pl.ds(pl.multiple_of(s * CAP, CAP), CAP)

    def several(one, s0, n):
        at_once = 5 if n % 5 == 0 else 4 if n % 4 == 0 else 3 if n % 3 == 0 else n

        def some(i, carry):
            for j in range(at_once):
                one(s0 + i * at_once + j)
            return carry

        lax.fori_loop(0, n // at_once, some, 0)

    def route(b, s0, n):
        for s in range(s0, s0 + n):
            if s > 0:
                df, dg = ORDER[s]
                share(b, dg, df).wait_recv()

        def weigh(s, carry):
            chosen = g[b, core, s, pl.ds(BODY, META), :].astype(F32)
            gate = g[b, other, s, pl.ds(BODY, META), :].astype(F32)
            for e in range(HELD):
                mine = (me * HELD + e).astype(F32)
                ws[s, pl.ds(e, 1), :] = jnp.sum(jnp.where(chosen == mine, gate, 0.0), axis=0, keepdims=True)
            return carry

        lax.fori_loop(s0, s0 + n, weigh, 0)
        w = ws[pl.ds(s0, n)].reshape(n * 8, TOKS)
        rank = jnp.dot((w > 0.0).astype(F32).astype(BF16), before, preferred_element_type=F32)
        ps[pl.ds(s0, n)] = jnp.where(w > 0.0, rank, -1.0).reshape(n, 8, TOKS)

        def one(s):
            r = ps[s]
            spread = jnp.concatenate(
                [jnp.where(jnp.broadcast_to(r[e:e + 1], (CAP, TOKS)) == cap_i, 1.0, 0.0) for e in range(HELD)],
                axis=0).astype(BF16)
            for j in range(8):
                k, c = (j // 4 + core) % 2, (j % 4) * 2
                pair = jnp.concatenate(
                    [g[b, k, s, pl.ds(c * 128, 128), :], g[b, k, s, pl.ds(c * 128 + 128, 128), :]], axis=1)
                picked = jnp.dot(spread, pair, preferred_element_type=F32).astype(BF16)
                for e in range(HELD):
                    xb[e, rows_of(s), pl.ds(j * 256, 256)] = picked[e * CAP:(e + 1) * CAP]

        several(one, s0, n)

    def expert(e0, n):
        def one(e, carry):
            rows = xb[e]
            gate_act = jnp.dot(rows, wg[e], preferred_element_type=F32)
            up_act = jnp.dot(rows, wu[e], preferred_element_type=F32)
            hidden = (gate_act / (1.0 + jnp.exp(-gate_act)) * up_act).astype(BF16)
            for j in range(4):
                xb[e, :, pl.ds(j * 512, 512)] = lax.dot_general(
                    hidden, wd[e, pl.ds(j * 512, 512), :], (((1,), (1,)), ((), ())),
                    preferred_element_type=F32).astype(BF16)
            return carry

        lax.fori_loop(e0, e0 + n, one, 0)

    returning = set()

    def back(b, df, dg):
        return remote(p.at[2, SLOT[df, dg]], g.at[b, 1, SLOT[dg, df], pl.ds(0, BODY), :],
                      ys.at[b], xr.at[b, SLOT[dg, df]], mate)

    def returned(b):
        remote(p.at[2], p.at[2], ys.at[b], xr.at[b, 0], mate).wait_send()

    def combine(b, s0, n):
        def one(s):
            r, w = ps[s], ws[s]
            mix = jnp.concatenate(
                [jnp.where(jnp.broadcast_to(r[e:e + 1], (CAP, TOKS)) == cap_i,
                           jnp.broadcast_to(w[e:e + 1], (CAP, TOKS)), 0.0) for e in range(HELD)], axis=0)
            mix = jnp.transpose(mix).astype(BF16)
            for j in range(8):
                k, c = (j // 4 + core) % 2, (j % 4) * 2
                res = jnp.concatenate([xb[e, rows_of(s), pl.ds(j * 256, 256)] for e in range(HELD)], axis=0)
                part = jnp.dot(mix, res, preferred_element_type=F32).astype(BF16)
                p[b + k * (2 - b), s, pl.ds(c * 128, 128), :] = part[:, :128]
                p[b + k * (2 - b), s, pl.ds(c * 128 + 128, 128), :] = part[:, 128:]

        several(one, s0, n)
        if b not in returning:
            pl.semaphore_wait(free_sem.at[b], 1)
        for s in range(s0, s0 + n):
            back(b, *ORDER[s]).start()
        returning.add(b)

    def mate_free(b):
        pl.semaphore_signal(free_sem.at[b], inc=1, device_id={"ep": mate}, device_id_type=MESH)

    def ready(b):
        for sem, n in ((ds, 15 if b else 14), (xs, 15)):
            blocks = g.at[b, 0, pl.ds(0, n)]
            remote(blocks, blocks, sem.at[b], dr.at[b, 0], mate).wait_send()
        for n in nbr.values():
            pl.semaphore_signal(ready_sem.at[b], inc=1, device_id={"ep": n}, device_id_type=MESH)

    home_ids = {}

    def hop(b, phase, df, kind):
        i = home_ids.setdefault((phase, df, kind), len(home_ids))
        step = 1 if kind[0] in "tp" else -1
        d = {"t": 2, "b": 2, "p": 1, "m": 3}[kind[0]]
        s = SLOT[(df, d) if phase == 1 else (d, 0)]
        a, n = RET[kind[-1]]
        land = (df * 3 if phase == 1 else 12) + {"t": 0, "b": 0, "p": 1, "m": 2}[kind[0]]
        return remote(p.at[b, s, pl.ds(a, n), :], g.at[b, 0, land, pl.ds(a, n), :],
                      rs.at[b], dr.at[b, i], nbr["g" if phase == 1 else "f", step])

    def home(*key):
        hop(*key).start()

    came = set()

    def total(b, df, dg, lands, parts="tb"):
        s = SLOT[df, dg]
        if (b, s) not in came:
            back(b, dg, df).wait_recv()
            came.add((b, s))
        for part in parts:
            a, n = RET[part]

            def add(i, carry):
                rows = pl.ds(pl.multiple_of(a + i * 128, 128), 128)
                v = p[b, s, rows, :].astype(F32) + g[b, 1, s, rows, :].astype(F32)
                for k in lands:
                    v = v + g[b, 0, k, rows, :].astype(F32)
                p[b, s, rows, :] = v.astype(BF16)
                return carry

            lax.fori_loop(0, n // 128, add, 0)

    def took(b, phase, df, *kinds):
        for kind in kinds:
            hop(b, phase, df, kind).wait_recv()

    def far(b, df):
        total(b, df, 2, [])
        home(b, 1, df, "t")
        home(b, 1, df, "b")

    def free(b, df):
        total(b, df, 1, [], "b")
        home(b, 1, df, "pb")
        total(b, df, 3, [], "t")
        home(b, 1, df, "mt")

    def near(b, df):
        took(b, 1, df, "t")
        total(b, df, 1, [df * 3], "t")
        home(b, 1, df, "pt")
        took(b, 1, df, "b")
        total(b, df, 3, [df * 3], "b")
        home(b, 1, df, "mb")

    def column(b, df, part):
        took(b, 1, df, "p" + part, "m" + part)
        lands = [df * 3 + 1, df * 3 + 2]
        if (df, part) in ((1, "t"), (3, "b")):
            took(b, 2, 2, part)
            lands.append(12)
        if df == 0:
            took(b, 2, 1, "p" + part)
            took(b, 2, 3, "m" + part)
            lands += [13, 14]
        total(b, df, 0, lands, part)
        if df:
            home(b, 2, df, {1: "p", 2: "", 3: "m"}[df] + part)

    def store(src, half):
        for c in range(8):
            out_ref[:, pl.ds(pl.multiple_of(half * HALF + c * 128, 128), 128)] = src[pl.ds(c * 128, 128), :]

    handover = remote(p.at[other, 0], fin, fs, fr, mate)

    def finish(b):
        column(b, 0, "t")
        column(b, 0, "b")

        @pl.when(core == b)
        def _():
            store(p.at[b, 0], core)

        @pl.when(core != b)
        def _():
            handover.start()

    for c in halves:
        c.wait_recv()
    first_ring(0)
    for key in early:
        leg(0, *key).wait_send()
    second_ring(0, 0)
    first_ring(1, 0)
    for c in loads:
        c.start()
    arrive(0, 1, 0)
    arrive(0, 3, 0)
    first_ring(1, 1)
    arrive(0, 0, 1)
    arrive(0, 0, 3)
    arrive(0, 2, 0)
    route(0, 0, 5)
    arrive(0, 1, 1)
    arrive(0, 1, 3)
    arrive(0, 3, 1)
    arrive(0, 3, 3)
    route(0, 5, 4)
    arrive(0, 2, 1)
    arrive(0, 2, 3)
    second_ring(1, 0)
    arrive(1, 1, 0)
    arrive(1, 3, 0)
    arrive(0, 0, 2)
    route(0, 9, 2)
    arrive(0, 1, 2)
    arrive(0, 3, 2)
    arrive(0, 2, 2)
    route(0, 11, 5)
    for c in halves:
        c.wait_send()
    mate_free(0)
    for c in loads:
        c.wait()
    expert(0, 1)
    arrive(1, 0, 1)
    arrive(1, 0, 3)
    arrive(1, 2, 0)
    expert(1, 1)
    ready(0)
    arrive(1, 1, 1)
    arrive(1, 1, 3)
    expert(2, 1)
    arrive(1, 3, 1)
    expert(3, 1)
    arrive(1, 3, 3)
    combine(0, 11, 5)
    combine(0, 9, 2)
    arrive(1, 2, 1)
    combine(0, 5, 4)
    arrive(1, 2, 3)
    arrive(1, 0, 2)
    pl.semaphore_wait(ready_sem.at[0], 4)
    far(0, 2)
    far(0, 1)
    free(0, 2)
    far(0, 3)
    combine(0, 0, 5)
    free(0, 1)
    far(0, 0)
    free(0, 3)
    free(0, 0)
    arrive(1, 1, 2)
    arrive(1, 3, 2)
    arrive(1, 2, 2)
    route(1, 0, 5)
    route(1, 5, 4)
    near(0, 2)
    route(1, 9, 7)
    mate_free(1)
    ready(1)
    expert(0, 2)
    near(0, 1)
    near(0, 3)
    expert(2, 1)
    near(0, 0)
    expert(3, 1)
    column(0, 2, "t")
    column(0, 2, "b")
    returned(0)
    combine(1, 11, 5)
    combine(1, 9, 2)
    combine(1, 5, 4)
    pl.semaphore_wait(ready_sem.at[1], 4)
    far(1, 2)
    far(1, 1)
    free(1, 2)
    far(1, 3)
    column(0, 1, "b")
    column(0, 3, "t")
    combine(1, 0, 5)
    free(1, 1)
    near(1, 2)
    column(0, 1, "t")
    column(0, 3, "b")
    far(1, 0)
    free(1, 3)
    near(1, 1)
    near(1, 3)
    column(1, 2, "t")
    column(1, 2, "b")
    free(1, 0)
    near(1, 0)
    finish(0)
    column(1, 1, "b")
    column(1, 3, "t")
    column(1, 1, "t")
    column(1, 3, "b")
    finish(1)
    handover.wait_recv()
    store(fin, other)
    returned(1)
    for b in range(2):
        sums = p.at[b, pl.ds(0, 15)]
        remote(sums, sums, rs.at[b], dr.at[b, 0], mate).wait_send()
    handover.wait_send()


def body(tokens, experts, gates, w_gate, w_up, w_down):
    dma, any_spec = pltpu.SemaphoreType.DMA, pl.BlockSpec(memory_space=pl.ANY)
    return pl.pallas_call(
        kernel,
        out_shape=pltpu.VMEM((TOKS, WIDTH), BF16),
        in_specs=[any_spec] * 6,
        out_specs=pl.BlockSpec(memory_space=pltpu.VMEM),
        scratch_shapes=[
            pltpu.VMEM((2, 2, CHIPS, ROWS, 128), BF16),
            pltpu.VMEM((3, CHIPS, BODY, 128), BF16),
            pltpu.VMEM((HELD, WIDTH, HIDDEN), BF16),
            pltpu.VMEM((HELD, WIDTH, HIDDEN), BF16),
            pltpu.VMEM((HELD, WIDTH, HIDDEN), BF16),
            pltpu.VMEM((HELD, CHIPS * CAP, WIDTH), BF16),
            pltpu.VMEM((CHIPS, 8, TOKS), F32),
            pltpu.VMEM((CHIPS, 8, TOKS), F32),
            pltpu.VMEM((BODY, 128), BF16),
            pltpu.VMEM((experts.shape[1], TOKS), jnp.int32),
            pltpu.VMEM((gates.shape[1], TOKS), BF16),
            pltpu.VMEM((2, META, TOKS), F32),
            dma((18,)), dma((3,)), dma((2,)), dma((2,)), dma((2,)),
            dma((2,)), dma((2, 30)), dma((2,)), dma((2, CHIPS)), dma((2,)), dma((2,)), dma, dma,
            pltpu.SemaphoreType.REGULAR((2,)), pltpu.SemaphoreType.REGULAR((2,)),
        ],
        compiler_params=pltpu.CompilerParams(
            collective_id=0, has_side_effects=True, vmem_limit_bytes=62000000),
    )(tokens, experts.T, gates.T, w_gate, w_up, w_down)


def solution(mesh):
    in_specs = (
        P(("rep", "ep"), None),
        P(("rep", "ep"), None),
        P(("rep", "ep"), None),
        P("ep", None, None),
        P("ep", None, None),
        P("ep", None, None),
    )
    out_specs = P(("rep", "ep"), None)
    return jax.shard_map(body, mesh=mesh, in_specs=in_specs, out_specs=out_specs, check_vma=False)
```

```python
import jax
import jax.numpy as jnp
from jax import lax
from jax.experimental import pallas as pl
from jax.experimental.pallas import tpu as pltpu
from jax.sharding import PartitionSpec as P

MESH = pl.DeviceIdType.MESH
F32, BF16 = jnp.float32, jnp.bfloat16
SIDE = 4
WIDTH, HIDDEN, TOKS, CAP, HELD = 2048, 512, 128, 16, 4
HALF = WIDTH // 2
BODY, META = 1024, 16
ROWS = BODY + META
SPANS = {"f": (0, ROWS), "t": (0, 528), "b": (528, 512)}
RET = {"f": (0, BODY), "t": (0, 512), "b": (512, 512)}
ORDER = [(0, 0), (1, 0), (3, 0), (0, 1), (0, 3), (1, 1), (1, 3), (3, 1),
         (3, 3), (2, 0), (0, 2), (2, 1), (2, 3), (1, 2), (3, 2), (2, 2)]
SLOT = {d: i for i, d in enumerate(ORDER)}
CHIPS = len(ORDER)


def kernel(tok_hbm, chosen_hbm, gates_hbm, wg_hbm, wu_hbm, wd_hbm, out_ref,
           g, p, wg, wu, wd, xb, ws, ps, fin,
           ids_v, gates_v, rows_v, own_sem, w_sem, os_, or_, es, ds, dr, xs, xr, ys, rs, fs, fr, free_sem, ready_sem):
    me = lax.axis_index("ep")
    core, x, y = me % 2, (me // 2) % SIDE, me // (2 * SIDE)
    other = 1 - core

    def at(cx, cy, c):
        return (cy * SIDE + cx) * 2 + c

    def pick(along_x, along_y):
        return other * along_x + core * along_y

    xp, xm = at((x + 1) % SIDE, y, core), at((x + SIDE - 1) % SIDE, y, core)
    yp, ym = at(x, (y + 1) % SIDE, core), at(x, (y + SIDE - 1) % SIDE, core)
    nbr = {("f", 1): pick(xp, yp), ("f", -1): pick(xm, ym), ("g", 1): pick(yp, xp), ("g", -1): pick(ym, xm)}
    mate = at(x, y, other)

    def remote(src, dst, send, recv, n):
        return pltpu.make_async_remote_copy(
            src_ref=src, dst_ref=dst, send_sem=send, recv_sem=recv, device_id={"ep": n}, device_id_type=MESH)

    barrier = pltpu.get_barrier_semaphore()
    for n in (*nbr.values(), mate):
        pl.semaphore_signal(barrier, inc=1, device_id={"ep": n}, device_id_type=MESH)

    own = []
    for k, half in ((0, core), (1, other)):
        for c in range(8):
            own.append(pltpu.make_async_copy(
                tok_hbm.at[:, pl.ds(pl.multiple_of(half * HALF + c * 128, 128), 128)],
                g.at[core, k, 0, pl.ds(c * 128, 128), :], own_sem.at[k * 9 + c]))
    routing = [pltpu.make_async_copy(chosen_hbm, ids_v, own_sem.at[8]), pltpu.make_async_copy(gates_hbm, gates_v, own_sem.at[17])]
    for c in (*routing, *own):
        c.start()
    loads = []
    for i, (src, dst) in enumerate(((wg_hbm, wg), (wu_hbm, wu), (wd_hbm, wd))):
        loads.append(pltpu.make_async_copy(src, dst, w_sem.at[i]))
    ws[...] = jnp.zeros_like(ws)
    topk = ids_v.shape[0]
    rows_v[0] = jnp.full((META, TOKS), -1.0, F32)
    rows_v[1] = jnp.zeros((META, TOKS), F32)
    for c in routing:
        c.wait()
    rows_v[0, pl.ds(0, topk), :] = ids_v[...].astype(F32)
    rows_v[1, pl.ds(0, topk), :] = gates_v[...].astype(F32)
    g[core, core, 0, pl.ds(BODY, META), :] = rows_v[0].astype(BF16)
    g[core, other, 0, pl.ds(BODY, META), :] = rows_v[1].astype(BF16)
    pl.semaphore_wait(barrier, 5)
    for c in own:
        c.wait()
    halves = [remote(g.at[core, 1 - k, 0], g.at[core, k, 0], os_.at[k], or_.at[k], mate) for k in range(2)]
    for c in halves:
        c.start()

    out_ids, early = {}, {(3, 0, "t"): 0, (1, 0, "b"): 1}

    def leg(b, df, dg, part):
        i = out_ids.setdefault((df, dg, part), len(out_ids))
        axis, d = ("f", df) if dg == 0 else ("g", dg)
        step = 1 if d == 3 or (d == 2 and part == "t") else -1
        prev = (d + step) % SIDE
        s = SLOT[(prev, 0) if dg == 0 else (df, prev)]
        a, n = SPANS[part]
        return remote(g.at[b, 0, s, pl.ds(a, n), :], g.at[b, 0, SLOT[df, dg], pl.ds(a, n), :],
                      es.at[early[df, dg, part]] if b == 0 and (df, dg, part) in early else ds.at[b],
                      dr.at[b, i], nbr[axis, step])

    def go(b, *key):
        leg(b, *key).start()

    def share(b, df, dg):
        return remote(g.at[b, 0, SLOT[df, dg]], g.at[b, 1, SLOT[dg, df]],
                      xs.at[b], xr.at[b, SLOT[dg, df]], mate)

    def second_ring(b, df):
        go(b, df, 3, "f")
        go(b, df, 1, "f")

    def first_ring(b, parts=2):
        if parts != 1:
            go(b, 3, 0, "t")
            go(b, 1, 0, "b")
        if parts != 0:
            go(b, 3, 0, "b")
            go(b, 1, 0, "t")

    def arrive(b, df, dg):
        if dg == 0:
            for part in ("b", "t") if df == 1 else ("t", "b"):
                leg(b, df, 0, part).wait_recv()
                if (df, part) in ((3, "t"), (1, "b")):
                    go(b, 2, 0, part)
            second_ring(b, df)
        else:
            for part in ("t", "b") if dg == 2 else ("f",):
                leg(b, df, dg, part).wait_recv()
            if dg != 2:
                go(b, df, 2, "t" if dg == 3 else "b")
        share(b, df, dg).start()

    row_i = lax.broadcasted_iota(jnp.int32, (TOKS, TOKS), 0)
    col_i = lax.broadcasted_iota(jnp.int32, (TOKS, TOKS), 1)
    before = (row_i < col_i).astype(F32).astype(BF16)
    cap_i = lax.broadcasted_iota(jnp.int32, (CAP, TOKS), 0).astype(F32)

    def rows_of(s):
        return pl.ds(pl.multiple_of(s * CAP, CAP), CAP)

    def several(one, s0, n):
        at_once = 5 if n % 5 == 0 else 4 if n % 4 == 0 else 3 if n % 3 == 0 else n

        def some(i, carry):
            for j in range(at_once):
                one(s0 + i * at_once + j)
            return carry

        lax.fori_loop(0, n // at_once, some, 0)

    def route(b, s0, n):
        for s in range(s0, s0 + n):
            if s > 0:
                df, dg = ORDER[s]
                share(b, dg, df).wait_recv()

        def weigh(s, carry):
            chosen = g[b, core, s, pl.ds(BODY, META), :].astype(F32)
            gate = g[b, other, s, pl.ds(BODY, META), :].astype(F32)
            for e in range(HELD):
                mine = (me * HELD + e).astype(F32)
                ws[s, pl.ds(e, 1), :] = jnp.sum(jnp.where(chosen == mine, gate, 0.0), axis=0, keepdims=True)
            return carry

        lax.fori_loop(s0, s0 + n, weigh, 0)
        w = ws[pl.ds(s0, n)].reshape(n * 8, TOKS)
        rank = jnp.dot((w > 0.0).astype(F32).astype(BF16), before, preferred_element_type=F32)
        ps[pl.ds(s0, n)] = jnp.where(w > 0.0, rank, -1.0).reshape(n, 8, TOKS)

        def one(s):
            r = ps[s]
            spread = jnp.concatenate(
                [jnp.where(jnp.broadcast_to(r[e:e + 1], (CAP, TOKS)) == cap_i, 1.0, 0.0) for e in range(HELD)],
                axis=0).astype(BF16)
            for j in range(8):
                k, c = (j // 4 + core) % 2, (j % 4) * 2
                pair = jnp.concatenate(
                    [g[b, k, s, pl.ds(c * 128, 128), :], g[b, k, s, pl.ds(c * 128 + 128, 128), :]], axis=1)
                picked = jnp.dot(spread, pair, preferred_element_type=F32).astype(BF16)
                for e in range(HELD):
                    xb[e, rows_of(s), pl.ds(j * 256, 256)] = picked[e * CAP:(e + 1) * CAP]

        several(one, s0, n)

    def expert(e0, n):
        def one(e, carry):
            rows = xb[e]
            gate_act = jnp.dot(rows, wg[e], preferred_element_type=F32)
            up_act = jnp.dot(rows, wu[e], preferred_element_type=F32)
            hidden = (gate_act / (1.0 + jnp.exp(-gate_act)) * up_act).astype(BF16)
            for j in range(4):
                xb[e, :, pl.ds(j * 512, 512)] = lax.dot_general(
                    hidden, wd[e, pl.ds(j * 512, 512), :], (((1,), (1,)), ((), ())),
                    preferred_element_type=F32).astype(BF16)
            return carry

        lax.fori_loop(e0, e0 + n, one, 0)

    returning = set()

    def back(b, df, dg):
        return remote(p.at[2, SLOT[df, dg]], g.at[b, 1, SLOT[dg, df], pl.ds(0, BODY), :],
                      ys.at[b], xr.at[b, SLOT[dg, df]], mate)

    def returned(b):
        remote(p.at[2], p.at[2], ys.at[b], xr.at[b, 0], mate).wait_send()

    def combine(b, s0, n):
        def one(s):
            r, w = ps[s], ws[s]
            mix = jnp.concatenate(
                [jnp.where(jnp.broadcast_to(r[e:e + 1], (CAP, TOKS)) == cap_i,
                           jnp.broadcast_to(w[e:e + 1], (CAP, TOKS)), 0.0) for e in range(HELD)], axis=0)
            mix = jnp.transpose(mix).astype(BF16)
            for j in range(8):
                k, c = (j // 4 + core) % 2, (j % 4) * 2
                res = jnp.concatenate([xb[e, rows_of(s), pl.ds(j * 256, 256)] for e in range(HELD)], axis=0)
                part = jnp.dot(mix, res, preferred_element_type=F32).astype(BF16)
                p[b + k * (2 - b), s, pl.ds(c * 128, 128), :] = part[:, :128]
                p[b + k * (2 - b), s, pl.ds(c * 128 + 128, 128), :] = part[:, 128:]

        several(one, s0, n)
        if b not in returning:
            pl.semaphore_wait(free_sem.at[b], 1)
        for s in range(s0, s0 + n):
            back(b, *ORDER[s]).start()
        returning.add(b)

    def mate_free(b):
        pl.semaphore_signal(free_sem.at[b], inc=1, device_id={"ep": mate}, device_id_type=MESH)

    def ready(b):
        for sem, n in ((ds, 15 if b else 14), (xs, 15)):
            blocks = g.at[b, 0, pl.ds(0, n)]
            remote(blocks, blocks, sem.at[b], dr.at[b, 0], mate).wait_send()
        for n in nbr.values():
            pl.semaphore_signal(ready_sem.at[b], inc=1, device_id={"ep": n}, device_id_type=MESH)

    home_ids = {}

    def hop(b, phase, df, kind):
        i = home_ids.setdefault((phase, df, kind), len(home_ids))
        step = 1 if kind[0] in "tp" else -1
        d = {"t": 2, "b": 2, "p": 1, "m": 3}[kind[0]]
        s = SLOT[(df, d) if phase == 1 else (d, 0)]
        a, n = RET[kind[-1]]
        land = (df * 3 if phase == 1 else 12) + {"t": 0, "b": 0, "p": 1, "m": 2}[kind[0]]
        return remote(p.at[b, s, pl.ds(a, n), :], g.at[b, 0, land, pl.ds(a, n), :],
                      rs.at[b], dr.at[b, i], nbr["g" if phase == 1 else "f", step])

    def home(*key):
        hop(*key).start()

    came = set()

    def total(b, df, dg, lands, parts="tb"):
        s = SLOT[df, dg]
        if (b, s) not in came:
            back(b, dg, df).wait_recv()
            came.add((b, s))
        for part in parts:
            a, n = RET[part]

            def add(i, carry):
                rows = pl.ds(pl.multiple_of(a + i * 128, 128), 128)
                v = p[b, s, rows, :].astype(F32) + g[b, 1, s, rows, :].astype(F32)
                for k in lands:
                    v = v + g[b, 0, k, rows, :].astype(F32)
                p[b, s, rows, :] = v.astype(BF16)
                return carry

            lax.fori_loop(0, n // 128, add, 0)

    def took(b, phase, df, *kinds):
        for kind in kinds:
            hop(b, phase, df, kind).wait_recv()

    def far(b, df):
        total(b, df, 2, [])
        home(b, 1, df, "t")
        home(b, 1, df, "b")

    def free(b, df):
        total(b, df, 1, [], "b")
        home(b, 1, df, "pb")
        total(b, df, 3, [], "t")
        home(b, 1, df, "mt")

    def near(b, df):
        took(b, 1, df, "t")
        total(b, df, 1, [df * 3], "t")
        home(b, 1, df, "pt")
        took(b, 1, df, "b")
        total(b, df, 3, [df * 3], "b")
        home(b, 1, df, "mb")

    def column(b, df, part):
        took(b, 1, df, "p" + part, "m" + part)
        lands = [df * 3 + 1, df * 3 + 2]
        if (df, part) in ((1, "t"), (3, "b")):
            took(b, 2, 2, part)
            lands.append(12)
        if df == 0:
            took(b, 2, 1, "p" + part)
            took(b, 2, 3, "m" + part)
            lands += [13, 14]
        total(b, df, 0, lands, part)
        if df:
            home(b, 2, df, {1: "p", 2: "", 3: "m"}[df] + part)

    def store(src, half):
        for c in range(8):
            out_ref[:, pl.ds(pl.multiple_of(half * HALF + c * 128, 128), 128)] = src[pl.ds(c * 128, 128), :]

    def handover(part):
        a, n = RET[part]
        i = "tb".index(part)
        return remote(p.at[other, 0, pl.ds(a, n), :], fin.at[pl.ds(a, n), :], fs.at[i], fr.at[i], mate)

    def finish(b):
        for part in "tb":
            column(b, 0, part)

            @pl.when(core != b)
            def _():
                handover(part).start()

        @pl.when(core == b)
        def _():
            store(p.at[b, 0], core)

    pl.when(core == 1)(halves[0].wait_recv)
    first_ring(0)
    for key in early:
        leg(0, *key).wait_send()
    second_ring(0, 0)
    pl.when(core == 0)(halves[0].wait_recv)
    halves[1].wait_recv()
    first_ring(1, 0)
    for c in loads:
        c.start()
    arrive(0, 1, 0)
    arrive(0, 3, 0)
    first_ring(1, 1)
    arrive(0, 0, 1)
    arrive(0, 0, 3)
    arrive(0, 2, 0)
    route(0, 0, 5)
    arrive(0, 1, 1)
    arrive(0, 1, 3)
    arrive(0, 3, 1)
    arrive(0, 3, 3)
    route(0, 5, 4)
    arrive(0, 2, 1)
    arrive(0, 2, 3)
    second_ring(1, 0)
    arrive(1, 1, 0)
    arrive(1, 3, 0)
    arrive(0, 0, 2)
    route(0, 9, 2)
    arrive(0, 1, 2)
    arrive(0, 3, 2)
    arrive(0, 2, 2)
    route(0, 11, 5)
    for c in halves:
        c.wait_send()
    mate_free(0)
    for c in loads:
        c.wait()
    expert(0, 1)
    arrive(1, 0, 1)
    arrive(1, 0, 3)
    arrive(1, 2, 0)
    expert(1, 1)
    ready(0)
    arrive(1, 1, 1)
    arrive(1, 1, 3)
    expert(2, 1)
    arrive(1, 3, 1)
    expert(3, 1)
    arrive(1, 3, 3)
    combine(0, 11, 5)
    combine(0, 9, 2)
    arrive(1, 2, 1)
    combine(0, 5, 4)
    arrive(1, 2, 3)
    arrive(1, 0, 2)
    pl.semaphore_wait(ready_sem.at[0], 4)
    far(0, 2)
    far(0, 1)
    free(0, 2)
    far(0, 3)
    combine(0, 0, 5)
    free(0, 1)
    far(0, 0)
    free(0, 3)
    free(0, 0)
    arrive(1, 1, 2)
    arrive(1, 3, 2)
    arrive(1, 2, 2)
    route(1, 0, 5)
    route(1, 5, 4)
    near(0, 2)
    route(1, 9, 7)
    mate_free(1)
    ready(1)
    expert(0, 2)
    near(0, 1)
    near(0, 3)
    expert(2, 1)
    near(0, 0)
    expert(3, 1)
    column(0, 2, "t")
    column(0, 2, "b")
    returned(0)
    combine(1, 11, 5)
    combine(1, 9, 2)
    combine(1, 5, 4)
    pl.semaphore_wait(ready_sem.at[1], 4)
    far(1, 2)
    far(1, 1)
    free(1, 2)
    far(1, 3)
    column(0, 1, "b")
    column(0, 3, "t")
    combine(1, 0, 5)
    free(1, 1)
    near(1, 2)
    column(0, 1, "t")
    column(0, 3, "b")
    far(1, 0)
    free(1, 3)
    near(1, 1)
    near(1, 3)
    column(1, 2, "t")
    column(1, 2, "b")
    free(1, 0)
    near(1, 0)
    finish(0)
    column(1, 1, "b")
    column(1, 3, "t")
    column(1, 1, "t")
    column(1, 3, "b")
    finish(1)
    for part in "tb":
        handover(part).wait_recv()
    store(fin, other)
    returned(1)
    for b in range(2):
        sums = p.at[b, pl.ds(0, 15)]
        remote(sums, sums, rs.at[b], dr.at[b, 0], mate).wait_send()
    for part in "tb":
        handover(part).wait_send()


def body(tokens, experts, gates, w_gate, w_up, w_down):
    dma, any_spec = pltpu.SemaphoreType.DMA, pl.BlockSpec(memory_space=pl.ANY)
    return pl.pallas_call(
        kernel,
        out_shape=pltpu.VMEM((TOKS, WIDTH), BF16),
        in_specs=[any_spec] * 6,
        out_specs=pl.BlockSpec(memory_space=pltpu.VMEM),
        scratch_shapes=[
            pltpu.VMEM((2, 2, CHIPS, ROWS, 128), BF16),
            pltpu.VMEM((3, CHIPS, BODY, 128), BF16),
            pltpu.VMEM((HELD, WIDTH, HIDDEN), BF16),
            pltpu.VMEM((HELD, WIDTH, HIDDEN), BF16),
            pltpu.VMEM((HELD, WIDTH, HIDDEN), BF16),
            pltpu.VMEM((HELD, CHIPS * CAP, WIDTH), BF16),
            pltpu.VMEM((CHIPS, 8, TOKS), F32),
            pltpu.VMEM((CHIPS, 8, TOKS), F32),
            pltpu.VMEM((BODY, 128), BF16),
            pltpu.VMEM((experts.shape[1], TOKS), jnp.int32),
            pltpu.VMEM((gates.shape[1], TOKS), BF16),
            pltpu.VMEM((2, META, TOKS), F32),
            dma((18,)), dma((3,)), dma((2,)), dma((2,)), dma((2,)),
            dma((2,)), dma((2, 30)), dma((2,)), dma((2, CHIPS)), dma((2,)), dma((2,)), dma((2,)), dma((2,)),
            pltpu.SemaphoreType.REGULAR((2,)), pltpu.SemaphoreType.REGULAR((2,)),
        ],
        compiler_params=pltpu.CompilerParams(
            collective_id=0, has_side_effects=True, vmem_limit_bytes=62000000),
    )(tokens, experts.T, gates.T, w_gate, w_up, w_down)


def solution(mesh):
    in_specs = (
        P(("rep", "ep"), None),
        P(("rep", "ep"), None),
        P(("rep", "ep"), None),
        P("ep", None, None),
        P("ep", None, None),
        P("ep", None, None),
    )
    out_specs = P(("rep", "ep"), None)
    return jax.shard_map(body, mesh=mesh, in_specs=in_specs, out_specs=out_specs, check_vma=False)
```
